256 devices in a mesh: gx: 8 (over y, core), gy: 32 (over x, z).
Axes of the slice: x: 4, y: 4, z: 8, core: 2. Of those that a mesh axis runs over, the one named last changes fastest.
Arguments:
- hidden_in: bfloat16 [8192, 2560], P(('gx', 'gy')), may hold values from -6 to 6
- norm_gain: float32 [2560], replicated, may hold values from 0.1 to 1.9
- router_weight: bfloat16 [2560, 64], replicated, may hold values from -0.0625 to 0.0625
- expert_ids: int32 [8192, 6], P(('gx', 'gy')), may hold values from 0 to 63, all different within a row; in each aligned block of 32 rows (0 to 31, 32 to 63, ...) at most 4 rows name the same one
- expert_gate: bfloat16 [64, 2560, 1536], P('gy', None, 'gx'), may hold values from -0.125 to 0.125
- expert_up: bfloat16 [64, 2560, 1536], P('gy', None, 'gx'), may hold values from -0.125 to 0.125
- expert_down: bfloat16 [64, 1536, 2560], P('gy', 'gx'), may hold values from -0.15625 to 0.15625
- shared_gate: bfloat16 [2560, 3072], P(None, 'gx'), may hold values from -0.125 to 0.125
- shared_up: bfloat16 [2560, 3072], P(None, 'gx'), may hold values from -0.125 to 0.125
- shared_down: bfloat16 [3072, 2560], P('gx'), may hold values from -0.109375 to 0.109375
- tree_kv: bfloat16 [8192, 1024], P(('gx', 'gy')), may hold values from -6 to 6
- accepted_path: int32 [256, 8], P(('gx', 'gy')), may hold values from 0 to 31, as said below
- accepted_len: int32 [256], P('gx'), may hold values from 1 to 8, as said below
- cache_owner: int32 [256], P('gx'), may hold values from 0 to 31, as said below
- owner_slot: int32 [256], P('gx'), may hold values from 0 to 8, as said below
Outputs:
- ffn_out: bfloat16 [8192, 2560], P(('gx', 'gy'))
- kept_kv: bfloat16 [4096, 1024], P(('gx', 'gy'))
The draws below stay inside these ranges and needn't reach their ends.
Inputs may be any that keep to these rules, and one draw needn't show every extreme that they name: `expert_ids`: each row names 6 different experts; within the rows of one device no expert is named by more than 4 rows, and that number is reached. `accepted_path`: each row is a path from the tree's root: strictly increasing tree positions, the first one 0. Only the first accepted_len[r] positions of row r of accepted_path are kept; some request keeps all 8. `cache_owner`: A request's cache lies on the device with the same index of gx and this index of gy; each such device holds the caches of exactly 2 requests of its index of gx, or of none. Requests with the same owner have disjoint ranges owner_slot to owner_slot + 7, which together cover the owner's 16 rows.
All inputs are finite; a program needn't handle non-finite values.
Results may differ from the reference program's by a relative error of at most 0.015.
Values may be sent and summed in bfloat16 or wider, within the bound.
A program may use at most 128 MiB of HBM per device.

```python
import math
import jax
import jax.numpy as jnp
import numpy as np
from jax import lax

D = 2560
FF = 1536
SHARED_FF = 3072
TOP = 6
REQ_DEV = 1
TREE = 32
ACCEPT = 8
EXPERTS = 64
FF_BLOCK = 192
TOK_DEV = 32
TOKENS = 8192
REQUESTS = 256
ROW_REQUESTS = 32
CAP = 4
KV_WIDTH = 1024
OWNER_ROWS = 16
KEPT_ROWS = 4096
N_GX = 8
N_GY = 32


def draw_accepted_path(key, part):
    path_keys = jax.random.split(key, REQUESTS)

    def one_path(path_key):
        chosen = jax.random.permutation(path_key, TREE - 1)[:ACCEPT - 1]
        descendants = jnp.sort(chosen).astype(jnp.int32) + 1
        return jnp.concatenate([jnp.zeros((1,), jnp.int32), descendants])
    return jax.vmap(one_path)(path_keys)


def draw_accepted_len(key, part):
    draw_key, high_key, low_key = jax.random.split(key, 3)
    lengths = jax.random.randint(draw_key, (REQUESTS,), 1, ACCEPT + 1).astype(jnp.int32)
    high_at = jax.random.randint(high_key, (), 0, REQUESTS)
    low_at = jax.random.randint(low_key, (), 0, REQUESTS)
    positions = jnp.arange(REQUESTS, dtype=jnp.int32)
    lengths = jnp.where(positions == low_at, 1, lengths)
    lengths = jnp.where(positions == high_at, ACCEPT, lengths)
    return lengths.astype(jnp.int32)


def owner_tables(key):
    base_key = jax.random.fold_in(key, 7177)
    row_count = REQUESTS // ROW_REQUESTS
    row_keys = jax.random.split(base_key, row_count)

    def one_row(row_key):
        rank_key, holder_key = jax.random.split(row_key)
        ranking = jax.random.permutation(rank_key, ROW_REQUESTS).astype(jnp.int32)
        holders = jax.random.permutation(holder_key, ROW_REQUESTS // REQ_DEV).astype(jnp.int32)
        groups = ranking // (2 * REQ_DEV)
        owners = jnp.take(holders, groups)
        slot_starts = ranking % (2 * REQ_DEV) * ACCEPT
        return (owners, slot_starts)
    owners, slot_starts = jax.vmap(one_row)(row_keys)
    return (owners.reshape(-1).astype(jnp.int32), slot_starts.reshape(-1).astype(jnp.int32))


def draw_cache_owner(key, part):
    owners, slot_starts = owner_tables(key)
    return owners


def draw_owner_slot(key, part):
    owners, slot_starts = owner_tables(key)
    return slot_starts


def levels(own_key, dims, pieces, least, high):
    factor_of, own = 1.0, jax.random.fold_in(own_key, 6)
    for axis_at, blocks in pieces:
        draws = jnp.exp(jax.random.uniform(jax.random.fold_in(own, axis_at), (blocks,), jnp.float32, least / len(pieces), high / len(pieces)))
        factor_of = factor_of * jnp.repeat(draws, dims[axis_at] // blocks).reshape([-1 if axis == axis_at else 1 for axis in range(len(dims))])
    return factor_of


def routed_block(key, own, number, rows, amount, top, limit, lean):
    sequence = jax.random.permutation(key, amount)
    heavy_load, common = load_shares(amount, rows * top, limit, lean, True), load_shares(amount, rows * top, limit, lean, False)
    places = jnp.arange(amount)

    def named(sizes, turn):
        used = int((sizes > 0).sum())
        fixed = max(1, used // 4)
        passed = fixed + (places - fixed + turn * (used - fixed)) % max(1, amount - fixed)
        return jnp.zeros((amount,), jnp.int32).at[sequence[jnp.where(places < fixed, places, passed)]].set(jnp.asarray(sizes, jnp.int32))

    sizes = jnp.where(number % 4 == 0, named(heavy_load, number // 4), named(common, number - number // 4 - 1))
    mixed = jax.random.permutation(jax.random.fold_in(own, 3), amount)
    donor, receiver = mixed[0:amount // 2 * 2:2], mixed[1:amount // 2 * 2:2]
    slack = jnp.minimum(sizes[donor] - 1, limit - sizes[receiver]) // 2
    slack = jnp.where((donor == sequence[0]) | (receiver == sequence[0]) | (sizes[receiver] == 0), 0, jnp.maximum(slack, 0))
    passed = jax.random.randint(jax.random.fold_in(own, 4), (amount // 2,), 0, 1 << 20) % (slack + 1)
    sizes = sizes.at[donor].add(-passed).at[receiver].add(passed)
    members = jnp.searchsorted(jnp.cumsum(sizes), jnp.arange(rows * top), side="right").astype(jnp.int32)
    table = members.reshape(top, rows).T
    table = table[jax.random.permutation(jax.random.fold_in(own, 1), rows)]
    turn = jax.random.randint(jax.random.fold_in(own, 2), (rows, 1), 0, top)
    return jnp.take_along_axis(table, (jnp.arange(top)[None, :] + turn) % top, axis=1)


def load_shares(count, total, reach, slope, full):
    weights = [(1 << 20) // math.isqrt(grade ** slope) + 1 for grade in range(1, count + 1)]
    largest = reach if full else min(reach, max(-(-total // count), total * weights[0] // sum(weights)))
    least = 1 if total - largest >= count - 1 else 0
    holding, rest = [largest] + [least] * (count - 1), total - largest - least * (count - 1)
    while rest > 0:
        movable = [i for i in range(1, count) if holding[i] < largest] or [i for i in range(1, count) if holding[i] < reach]
        pool, budget = sum([weights[i] for i in movable]), rest
        for i in movable:
            extra = min(reach - holding[i], max(1, budget * weights[i] // pool), rest)
            holding[i] = holding[i] + extra
            rest = rest - extra
    return np.array(holding)


def noise(key, shape, width, most, cuts=(), held_as=jnp.bfloat16):
    drawn = jax.random.normal(key, shape, jnp.float32) * width
    if len(cuts) > 0:
        drawn = levels(key, shape, cuts, -0.22, 0.18) * drawn
    return jnp.clip(drawn, min=-most, max=most).astype(held_as)


def setup_inputs(seed: int = 0) -> dict:
    streams_of = jax.random.split(jax.random.key(seed), 16)
    hidden_in = noise(streams_of[0], (TOKENS, D), 1.0, 6.0, ((0, 256),))
    norm_gain = jnp.clip(1.0 + 0.18 * jax.random.normal(streams_of[1], (D,), jnp.float32), 0.1, 1.9)
    router_weight = noise(streams_of[2], (D, EXPERTS), (4 * D) ** -0.5, 0.0625)
    expert_ids_keys = jax.random.split(jax.random.fold_in(streams_of[3], 1), TOKENS // TOK_DEV)
    expert_ids_turns = jax.random.permutation(jax.random.fold_in(streams_of[3], 3), TOKENS // TOK_DEV)
    expert_ids = jax.vmap(lambda own, number: routed_block(jax.random.fold_in(streams_of[3], 2), own, number, TOK_DEV, EXPERTS, TOP, CAP, 2))(expert_ids_keys, expert_ids_turns).reshape((TOKENS, TOP))
    expert_gate = noise(streams_of[4], (EXPERTS, D, FF), D ** -0.5, 0.125, ((0, 32), (2, 8)))
    expert_up = noise(streams_of[5], (EXPERTS, D, FF), D ** -0.5, 0.125, ((0, 32), (2, 8)))
    expert_down = noise(streams_of[6], (EXPERTS, FF, D), FF ** -0.5, 0.15625, ((0, 32), (1, 8)))
    shared_gate = noise(streams_of[7], (D, SHARED_FF), D ** -0.5, 0.125, ((1, 8),))
    shared_up = noise(streams_of[8], (D, SHARED_FF), D ** -0.5, 0.125, ((1, 8),))
    shared_down = noise(streams_of[9], (SHARED_FF, D), SHARED_FF ** -0.5, 0.109375, ((0, 8),))
    tree_kv = noise(streams_of[10], (TOKENS, KV_WIDTH), 1.0, 6.0, ((0, 256),))
    accepted_path = draw_accepted_path(jax.random.fold_in(streams_of[15], 71), 0)
    accepted_len = draw_accepted_len(jax.random.fold_in(streams_of[15], 71), 0)
    cache_owner = draw_cache_owner(jax.random.fold_in(streams_of[15], 71), 0)
    owner_slot = draw_owner_slot(jax.random.fold_in(streams_of[15], 71), 0)
    return {"hidden_in": hidden_in, "norm_gain": norm_gain, "router_weight": router_weight, "expert_ids": expert_ids, "expert_gate": expert_gate, "expert_up": expert_up, "expert_down": expert_down, "shared_gate": shared_gate, "shared_up": shared_up, "shared_down": shared_down, "tree_kv": tree_kv, "accepted_path": accepted_path, "accepted_len": accepted_len, "cache_owner": cache_owner, "owner_slot": owner_slot}


epsilon = 1e-05

def reference(hidden_in, norm_gain, router_weight, expert_ids, expert_gate, expert_up, expert_down, shared_gate, shared_up, shared_down, tree_kv, accepted_path, accepted_len, cache_owner, owner_slot):
    widened = hidden_in.astype(jnp.float32)
    scale_inv = lax.rsqrt(lax.optimization_barrier(jnp.mean(widened * widened, axis=-1, keepdims=True)) + epsilon)
    normed = (widened * scale_inv * norm_gain).astype(jnp.bfloat16)
    scores = jax.nn.sigmoid(jnp.dot(normed, router_weight, preferred_element_type=jnp.float32))
    picked = jnp.take_along_axis(scores, expert_ids, axis=1)
    gate_values = (picked / lax.optimization_barrier(jnp.sum(picked, axis=1, keepdims=True))).astype(jnp.bfloat16)
    chosen = expert_ids[:, :, None] == jnp.arange(EXPERTS, dtype=jnp.int32)
    routed_mask = jnp.any(chosen, axis=1).astype(jnp.int32)
    block_count = TOKENS // TOK_DEV
    places = (jnp.cumsum(routed_mask.reshape(block_count, TOK_DEV, EXPERTS), axis=1) - 1).astype(jnp.int32)
    places = places.reshape(TOKENS, EXPERTS)
    place_of = jnp.take_along_axis(places, expert_ids, axis=1).astype(jnp.int32)
    token_index = jnp.arange(TOKENS, dtype=jnp.int32)
    slot_of = ((token_index // TOK_DEV)[:, None] * CAP + place_of).astype(jnp.int32)
    slot_total = block_count * CAP
    source = jnp.full((EXPERTS, slot_total), TOKENS, jnp.int32)
    source = source.at[expert_ids, slot_of].set(jnp.broadcast_to(token_index[:, None], expert_ids.shape))
    padded = jnp.concatenate([normed, jnp.zeros((1, D), jnp.bfloat16)], axis=0)

    def one_expert(operands):
        rows_src, weight_gate, weight_up, weight_down = operands
        rows_in = jnp.take(padded, rows_src, axis=0)
        gate_out = jnp.dot(rows_in, weight_gate, preferred_element_type=jnp.float32)
        up_out = jnp.dot(rows_in, weight_up, preferred_element_type=jnp.float32)
        hidden = (jax.nn.silu(gate_out) * up_out).astype(jnp.bfloat16)
        hidden_blocks = hidden.reshape(slot_total, N_GX, FF_BLOCK).astype(jnp.float32)
        down_blocks = weight_down.reshape(N_GX, FF_BLOCK, D).astype(jnp.float32)
        partial_value = jnp.einsum('snf,nfd->snd', hidden_blocks, down_blocks, precision=lax.Precision.HIGHEST).astype(jnp.bfloat16)
        return lax.optimization_barrier(jnp.sum(partial_value.astype(jnp.float32), axis=1))
    expert_out = lax.map(one_expert, (source, expert_gate, expert_up, expert_down))
    routed = jnp.zeros((TOKENS, D), jnp.float32)
    for rank_idx in range(TOP):
        fetched = expert_out[expert_ids[:, rank_idx], slot_of[:, rank_idx]]
        routed = routed + gate_values[:, rank_idx].astype(jnp.float32)[:, None] * fetched
    shared_gate_out = jnp.dot(normed, shared_gate, preferred_element_type=jnp.float32)
    shared_up_out = jnp.dot(normed, shared_up, preferred_element_type=jnp.float32)
    shared_hidden = (jax.nn.silu(shared_gate_out) * shared_up_out).astype(jnp.bfloat16)
    shared = jnp.dot(shared_hidden, shared_down, preferred_element_type=jnp.float32)
    ffn_out = (routed + shared).astype(jnp.bfloat16)
    request_index = jnp.arange(REQUESTS, dtype=jnp.int32)
    row_of = request_index // ROW_REQUESTS
    steps_along = jnp.arange(ACCEPT, dtype=jnp.int32)
    valid = steps_along[None, :] < accepted_len[:, None]
    start_row = (row_of * N_GY + cache_owner) * OWNER_ROWS + owner_slot
    target = jnp.where(valid, start_row[:, None] + steps_along[None, :], KEPT_ROWS).astype(jnp.int32)
    path_rows = jnp.take(tree_kv, ((request_index * TREE)[:, None] + accepted_path).reshape(-1), axis=0)
    kept_kv = jnp.zeros((KEPT_ROWS, KV_WIDTH), jnp.bfloat16).at[target.reshape(-1)].set(path_rows, mode='drop')
    return (ffn_out, kept_kv)
```

```python
import jax
import jax.numpy as jnp
from jax import lax
from jax.experimental import pallas as pl
from jax.experimental.pallas import tpu as pltpu
from jax.sharding import PartitionSpec as P

NX, NY, NZ = 4, 4, 8
D = 2560
FFB = 192
SFB = 384
TOK = 32
EXPERTS = 64
META = 128
KVW = 1024
KVL = 256
ROW = D + META + KVL
COLS = 512
EPSILON = 1e-05
BF = jnp.bfloat16
F32 = jnp.float32
MESH = pl.DeviceIdType.MESH
COPIES = 128


def mm(a, b):
    return jnp.dot(a, b, preferred_element_type=F32)


def onehot(cond):
    return jnp.where(cond, 1.0, 0.0).astype(BF)


def iota(shape, dim):
    return lax.broadcasted_iota(jnp.int32, shape, dim)


def kernel(
    hidden, gain, router, ids, path, lens, owner, slot, tree,
    eg, eu, ed, sg, su, sd,
    out, kept,
    zbuf, xsend, ag, outb, rl, rs, sret, ret, ohg, comb, zl, zr,
    shb, outs, rls, rss, hid, hids, kvs, kvr,
    wg0, wu0, wd0, vg0, vu0, vd0, wg1, wu1, wd1, vg1, vu1, vd1,
    send_sem, recv_sem, local_sem,
):
    gx, gy = lax.axis_index("gx"), lax.axis_index("gy")
    y, c = gx // 2, gx % 2
    x, z = gy // NZ, gy % NZ
    zp = (gx, x * NZ + (z + 1) % NZ)
    zm = (gx, x * NZ + (z + NZ - 1) % NZ)
    xp = (gx, (x + 1) % NX * NZ + z)
    xm = (gx, (x + NX - 1) % NX * NZ + z)
    x2 = (gx, (x + 2) % NX * NZ + z)
    yp = ((y + 1) % NY * 2 + c, gy)
    ym = ((y + NY - 1) % NY * 2 + c, gy)
    mate = (y * 2 + 1 - c, gy)

    started = []

    def send(src, dst, device):
        number = len(started)
        copy = pltpu.make_async_remote_copy(
            src_ref=src, dst_ref=dst,
            send_sem=send_sem.at[number], recv_sem=recv_sem.at[number],
            device_id=device, device_id_type=MESH,
        )
        copy.start()
        started.append(copy)
        return copy

    own = []
    for k, (src, dst) in enumerate(
        ((sg, vg0), (su, vu0), (sd, vd0), (eg, wg0), (eu, wu0), (ed, wd0))
    ):
        copy = pltpu.make_async_copy(src, dst, local_sem.at[k])
        copy.start()
        own.append(copy)

    barrier = pltpu.get_barrier_semaphore()
    for device in (zp, zm, xp, xm, x2, yp, ym, mate):
        pl.semaphore_signal(barrier, inc=1, device_id=device, device_id_type=MESH)

    wide = hidden[...].astype(F32)
    scale = lax.rsqrt(jnp.mean(wide * wide, axis=-1, keepdims=True) + EPSILON)
    normed = (wide * scale * gain[...]).astype(BF)
    zbuf[0:TOK, 0:D] = normed
    shb[0:TOK, :] = normed
    scores = 1.0 / (1.0 + jnp.exp(-mm(normed, router[...])))
    lane = iota((TOK, EXPERTS), 1)
    chosen = lane == ids[:, 0:1]
    for k in range(1, ids.shape[1]):
        chosen = chosen | (lane == ids[:, k:k + 1])
    picked = jnp.where(chosen, scores, 0.0)
    gates = (picked / jnp.sum(picked, axis=-1, keepdims=True)).astype(BF)
    low = iota((EXPERTS, META), 1)
    high = iota((EXPERTS, META), 0)
    meta = mm(gates, onehot(low == high)) + mm(onehot(chosen), onehot(low == high + EXPERTS))
    zbuf[0:TOK, D:D + META] = meta.astype(BF)
    row = iota((TOK, 8), 0)
    steps = jnp.sum(
        jnp.where(row // 4 == iota((TOK, 8), 1), path[...].astype(F32), 0.0), axis=1, keepdims=True
    )
    square_row, square_lane = iota((TOK, TOK), 0), iota((TOK, TOK), 1)
    on_path = square_lane.astype(F32) == steps
    rows_kv = jnp.zeros((TOK, KVL), F32)
    for q in range(4):
        rows_kv += mm(onehot(on_path & (square_row % 4 == q)), tree[:, q * KVL:(q + 1) * KVL])
    zbuf[0:TOK, D + META:ROW] = rows_kv.astype(BF)

    pl.semaphore_wait(barrier, 8)

    right, left = {}, {}

    def hop(h):
        for ch in range(2):
            lo = ch * 16
            if h < 4 or ch == 0:
                if h > 1:
                    right[h - 1, ch].wait_recv()
                right[h, ch] = send(
                    zbuf.at[pl.ds((h - 1) * TOK + lo, 16), :], zbuf.at[pl.ds(h * TOK + lo, 16), :], zp
                )
            if h < 4 or ch == 1:
                if h > 1:
                    left[h - 1, ch].wait_recv()
                left[h, ch] = send(
                    zbuf.at[pl.ds((NZ - h + 1) % NZ * TOK + lo, 16), :],
                    zbuf.at[pl.ds((NZ - h) * TOK + lo, 16), :], zm,
                )

    hop(1)
    tokens = zbuf.at[pl.ds(0, TOK), pl.ds(0, D)]
    sh_p = send(tokens, shb.at[pl.ds(TOK, TOK), :], yp)
    sh_m = send(tokens, shb.at[pl.ds(2 * TOK, TOK), :], ym)
    other = [
        send(src, dst, mate)
        for src, dst in ((sg, vg1), (su, vu1), (sd, vd1), (eg, wg1), (eu, wu1), (ed, wd1))
    ]
    hop(2)
    sh_p.wait_recv()
    sh_p2 = send(shb.at[pl.ds(TOK, 16), :], shb.at[pl.ds(3 * TOK, 16), :], yp)
    sh_m.wait_recv()
    sh_m2 = send(shb.at[pl.ds(2 * TOK + 16, 16), :], shb.at[pl.ds(3 * TOK + 16, 16), :], ym)
    hop(3)
    hop(4)
    right[3, 1].wait_recv()
    left[3, 0].wait_recv()
    right[4, 0].wait_recv()
    left[4, 1].wait_recv()

    rows = NZ * TOK
    pair = iota((16, META), 0) % 8
    step = pair // 2
    turn = jnp.where(step == 2, 3, jnp.where(step == 3, 2, step))
    expert = 2 * ((x + turn) % NX * NZ + z) + pair % 2
    meta_lane = iota((16, META), 1)
    all_meta = zbuf[:, D:D + META]
    along = (((1,), (1,)), ((), ()))
    gate_of = lax.dot_general(onehot(meta_lane == expert), all_meta, along, preferred_element_type=F32)
    mask_of = lax.dot_general(
        onehot(meta_lane == expert + EXPERTS), all_meta, along, preferred_element_type=F32
    )
    big_row, big_lane = iota((rows, rows), 0), iota((rows, rows), 1)
    before = onehot((big_row < big_lane) & (big_row // TOK == big_lane // TOK))
    place = mm(mask_of.astype(BF), before)
    key = jnp.where(mask_of > 0.5, place, -1.0)
    slot_row, slot_lane = iota((TOK, rows), 0), iota((TOK, rows), 1)
    block = slot_lane // TOK == slot_row // 4
    seat = (slot_row % 4).astype(F32)

    def slots(i):
        parts = []
        for l in range(2):
            j = 2 * i + l
            here = block & (key[j:j + 1, :] == seat)
            ohg[pl.ds(j * TOK, TOK), :] = jnp.where(here, gate_of[j:j + 1, :], 0.0).astype(BF)
            parts.append(onehot(here))
        return jnp.concatenate(parts, axis=0)

    sent_x = {}
    for i, device in ((3, x2), (1, xp), (2, xm), (0, None)):
        table = slots(i)

        @pl.loop(0, D // COLS)
        def _(n):
            cols = pl.ds(pl.multiple_of(n * COLS, COLS), COLS)
            value = mm(table, zbuf[:, cols]).astype(BF)
            for l in range(2):
                part = value[l * TOK:(l + 1) * TOK, :]
                if i:
                    xsend[i - 1, l, :, cols] = part
                else:
                    ag[l, 0:TOK, cols] = part

        if i:
            for l in range(2):
                sent_x[i, l] = send(xsend.at[i - 1, l], ag.at[l, pl.ds(i * TOK, TOK), :], device)

    direct, relay = {}, {}

    def spread(j):
        for l in range(2):
            here = ag.at[l, pl.ds(j * TOK, TOK), :]
            direct[j, l, 0] = send(here, ag.at[l, pl.ds((NX + j) * TOK, TOK), :], yp)
            direct[j, l, 1] = send(here, ag.at[l, pl.ds((2 * NX + j) * TOK, TOK), :], ym)

    def pass_on(j):
        far = 3 * NX + j
        direct[j, 0, 0].wait_recv()
        relay[j, 0] = send(
            ag.at[0, pl.ds((NX + j) * TOK, TOK), :], ag.at[0, pl.ds(far * TOK, TOK), :], yp
        )
        direct[j, 1, 1].wait_recv()
        relay[j, 1] = send(
            ag.at[1, pl.ds((2 * NX + j) * TOK, TOK), :], ag.at[1, pl.ds(far * TOK, TOK), :], ym
        )

    spread(0)

    kv_row, kv_lane = iota((TOK, rows), 0), iota((TOK, rows), 1)
    spreader = onehot(kv_row == NZ * x + (z + NZ - kv_lane // TOK) % NZ)

    def per_lane(ref):
        return mm(jnp.broadcast_to(ref[...].astype(F32), (16, TOK)).astype(BF), spreader)[0:1, :]

    own_v, slot_v, len_v = per_lane(owner), per_lane(slot), per_lane(lens)
    pick_row, pick_lane = iota((64, rows), 0), iota((64, rows), 1)
    kv_step = pick_row // 16
    kv_turn = jnp.where(kv_step == 2, 3, jnp.where(kv_step == 3, 2, kv_step))
    target = ((x + kv_turn) % NX * NZ + z).astype(F32)
    depth = (pick_lane % TOK // 4).astype(F32)
    wanted = (own_v == target) & (slot_v + depth == (pick_row % 16).astype(F32)) & (depth < len_v)
    for q in range(4):
        value = mm(onehot(wanted & (pick_lane % 4 == q)), zbuf[:, D + META:ROW]).astype(BF)
        for i in range(4):
            kvs[i, :, q * KVL:(q + 1) * KVL] = value[i * 16:(i + 1) * 16, :]
    sent_kv = [
        send(kvs.at[i], kvr.at[i - 1], device) for i, device in ((1, xp), (2, xm), (3, x2))
    ]

    sh_p2.wait_recv()
    sh_m2.wait_recv()
    for k in range(3):
        own[k].wait()
        other[k].wait_recv()

    def silu_mul(g, u):
        return (g / (1.0 + jnp.exp(-g)) * u).astype(BF)

    for h, (vg, vu) in enumerate(((vg0, vu0), (vg1, vu1))):
        hids[h] = silu_mul(mm(shb[...], vg[...]), mm(shb[...], vu[...]))

    @pl.loop(0, D // COLS)
    def _(n):
        cols = pl.ds(pl.multiple_of(n * COLS, COLS), COLS)
        outs[:, cols] = (mm(hids[0], vd0[:, cols]) + mm(hids[1], vd1[:, cols])).astype(BF)

    far_p = send(outs.at[pl.ds(3 * TOK, 16), :], rls.at[0], yp)
    far_m = send(outs.at[pl.ds(3 * TOK + 16, 16), :], rls.at[1], ym)

    for l in range(2):
        sent_x[1, l].wait_recv()
    spread(1)
    pass_on(0)
    for l in range(2):
        sent_x[2, l].wait_recv()
    spread(2)
    pass_on(1)
    for l in range(2):
        sent_x[3, l].wait_recv()
    spread(3)
    far_p.wait_recv()
    outs[2 * TOK:2 * TOK + 16, :] = (
        outs[2 * TOK:2 * TOK + 16, :].astype(F32) + rls[0].astype(F32)
    ).astype(BF)
    far_m.wait_recv()
    outs[TOK + 16:2 * TOK, :] = (
        outs[TOK + 16:2 * TOK, :].astype(F32) + rls[1].astype(F32)
    ).astype(BF)
    back_p = send(outs.at[pl.ds(2 * TOK, TOK), :], rss.at[0], yp)
    back_m = send(outs.at[pl.ds(TOK, TOK), :], rss.at[1], ym)
    pass_on(2)
    pass_on(3)
    for k in range(3, 6):
        own[k].wait()
        other[k].wait_recv()
    for j in range(4):
        direct[j, 1, 0].wait_recv()
        direct[j, 0, 1].wait_recv()

    def routed(first, count):
        @pl.loop(0, 2)
        def _(l):
            for h, (wg, wu) in enumerate(((wg0, wu0), (wg1, wu1))):
                value = ag[l, first:first + count, :]
                hid[h, 0:count, :] = silu_mul(mm(value, wg[l]), mm(value, wu[l]))

            @pl.loop(0, D // COLS)
            def _(n):
                cols = pl.ds(pl.multiple_of(n * COLS, COLS), COLS)
                outb[l, first:first + count, cols] = (
                    mm(hid[0, 0:count, :], wd0[l, :, cols]) + mm(hid[1, 0:count, :], wd1[l, :, cols])
                ).astype(BF)

    span = NX * TOK
    routed(0, 3 * span)
    plain_p = send(outb.at[1, pl.ds(2 * span, span), :], rs.at[0, 1], yp)
    plain_m = send(outb.at[0, pl.ds(span, span), :], rs.at[1, 0], ym)
    for j in range(4):
        relay[j, 0].wait_recv()
        relay[j, 1].wait_recv()
    routed(3 * span, span)

    order = (3, 1, 2, 0)
    far = {}
    for j in order:
        rows_j = pl.ds(3 * span + j * TOK, TOK)
        far[j, 0] = send(outb.at[0, rows_j, :], rl.at[0, pl.ds(j * TOK, TOK), :], yp)
        far[j, 1] = send(outb.at[1, rows_j, :], rl.at[1, pl.ds(j * TOK, TOK), :], ym)
    back = {}
    sent_back = {}

    def add_far(j):
        lo = j * TOK
        for l, base, device in ((0, 2 * span, yp), (1, span, ym)):
            far[j, l].wait_recv()
            outb[l, base + lo:base + lo + TOK, :] = (
                outb[l, base + lo:base + lo + TOK, :].astype(F32) + rl[l, lo:lo + TOK, :].astype(F32)
            ).astype(BF)
            back[j, l] = send(
                outb.at[l, pl.ds(base + lo, TOK), :], rs.at[l, l, pl.ds(lo, TOK), :], device
            )

    def finish(j, device):
        lo = j * TOK
        for l in range(2):
            back[j, l].wait_recv()
        for l in range(2):
            total = (
                outb[l, lo:lo + TOK, :].astype(F32)
                + rs[0, l, lo:lo + TOK, :].astype(F32)
                + rs[1, l, lo:lo + TOK, :].astype(F32)
            ).astype(BF)
            if j:
                sret[l, lo:lo + TOK, :] = total
                sent_back[j, l] = send(
                    sret.at[l, pl.ds(lo, TOK), :], ret.at[pl.ds((2 * j + l) * TOK, TOK), :], device
                )
            else:
                ret[l * TOK:(l + 1) * TOK, :] = total

    goes = {0: None, 1: xm, 2: xp, 3: x2}
    add_far(3)
    plain_p.wait_recv()
    plain_m.wait_recv()
    add_far(1)
    finish(3, goes[3])
    add_far(2)
    finish(1, goes[1])
    add_far(0)
    finish(2, goes[2])
    finish(0, goes[0])
    for copy in sent_back.values():
        copy.wait_recv()

    across = (((0,), (0,)), ((), ()))

    def combine(k):
        weights = ohg[:, k * TOK:(k + 1) * TOK]

        @pl.loop(0, D // COLS)
        def _(n):
            cols = pl.ds(pl.multiple_of(n * COLS, COLS), COLS)
            comb[k * TOK:(k + 1) * TOK, cols] = lax.dot_general(
                weights, ret[:, cols], across, preferred_element_type=F32
            ).astype(BF)

    for k in range(NZ):
        combine(k)
    go_l, go_r = {}, {}
    for h in range(1, 5):
        for ch in range(2):
            lo = ch * 16
            for flow, going, buf, k, device in (
                (0, go_l, zl, 5 - h, zm), (1, go_r, zr, 3 + h, zp)
            ):
                if h == 1 and ch == flow:
                    continue
                at = k * TOK + lo
                if (h - 1, ch) in going:
                    going[h - 1, ch].wait_recv()
                    comb[at:at + 16, :] = (
                        comb[at:at + 16, :].astype(F32) + buf[h - 2, lo:lo + 16, :].astype(F32)
                    ).astype(BF)
                going[h, ch] = send(
                    comb.at[pl.ds(at, 16), :], buf.at[h - 1, pl.ds(lo, 16), :], device
                )

    back_p.wait_recv()
    back_m.wait_recv()
    for copy in sent_kv:
        copy.wait_recv()
    kept[...] = (
        kvs[0].astype(F32) + kvr[0].astype(F32) + kvr[1].astype(F32) + kvr[2].astype(F32)
    ).astype(BF)
    total = outs[0:TOK, :].astype(F32) + rss[0].astype(F32) + rss[1].astype(F32)
    total = total + comb[0:TOK, :].astype(F32)
    for ch in range(2):
        go_l[4, ch].wait_recv()
        go_r[4, ch].wait_recv()
    out[...] = (total + zl[3].astype(F32) + zr[3].astype(F32)).astype(BF)
    for copy in started:
        copy.wait_send()


def shards(
    hidden_in, norm_gain, router_weight, expert_ids, expert_gate, expert_up, expert_down,
    shared_gate, shared_up, shared_down, tree_kv, accepted_path, accepted_len, cache_owner, owner_slot,
):
    vmem = pl.BlockSpec(memory_space=pltpu.VMEM)
    hbm = pl.BlockSpec(memory_space=pl.ANY)
    V = pltpu.VMEM
    span = NX * TOK
    scratch = [
        V((NZ * TOK, ROW), BF),
        V((3, 2, TOK, D), BF),
        V((2, NY * span, D), BF),
        V((2, NY * span, D), BF),
        V((2, span, D), BF),
        V((2, 2, span, D), BF),
        V((2, span, D), BF),
        V((2 * span, D), BF),
        V((2 * span, NZ * TOK), BF),
        V((NZ * TOK, D), BF),
        V((4, TOK, D), BF),
        V((4, TOK, D), BF),
        V((NY * TOK, D), BF),
        V((NY * TOK, D), BF),
        V((2, 16, D), BF),
        V((2, TOK, D), BF),
        V((2, 3 * span, FFB), BF),
        V((2, NY * TOK, SFB), BF),
        V((4, 16, KVW), BF),
        V((3, 16, KVW), BF),
    ]
    for _ in range(2):
        scratch += [
            V((2, D, FFB), BF), V((2, D, FFB), BF), V((2, FFB, D), BF),
            V((D, SFB), BF), V((D, SFB), BF), V((SFB, D), BF),
        ]
    scratch += [
        pltpu.SemaphoreType.DMA((COPIES,)),
        pltpu.SemaphoreType.DMA((COPIES,)),
        pltpu.SemaphoreType.DMA((6,)),
    ]
    return pl.pallas_call(
        kernel,
        name="verify_ffn",
        out_shape=(
            jax.ShapeDtypeStruct((TOK, D), BF),
            jax.ShapeDtypeStruct((16, KVW), BF),
        ),
        in_specs=[vmem] * 9 + [hbm] * 6,
        out_specs=(vmem, vmem),
        scratch_shapes=scratch,
        compiler_params=pltpu.CompilerParams(
            collective_id=0, has_side_effects=True, vmem_limit_bytes=62 * 1024 * 1024
        ),
    )(
        hidden_in, norm_gain.reshape(1, D), router_weight, expert_ids, accepted_path,
        accepted_len.reshape(1, TOK), cache_owner.reshape(1, TOK), owner_slot.reshape(1, TOK), tree_kv,
        expert_gate, expert_up, expert_down, shared_gate, shared_up, shared_down,
    )


def solution(mesh):
    in_specs = (
        P(("gx", "gy"), None),
        P(),
        P(),
        P(("gx", "gy"), None),
        P("gy", None, "gx"),
        P("gy", None, "gx"),
        P("gy", "gx", None),
        P(None, "gx"),
        P(None, "gx"),
        P("gx", None),
        P(("gx", "gy"), None),
        P(("gx", "gy"), None),
        P("gx"),
        P("gx"),
        P("gx"),
    )
    out_specs = (P(("gx", "gy"), None), P(("gx", "gy"), None))
    return jax.shard_map(shards, mesh=mesh, in_specs=in_specs, out_specs=out_specs, check_vma=False)
```

```python
import jax
import jax.numpy as jnp
from jax import lax
from jax.experimental import pallas as pl
from jax.experimental.pallas import tpu as pltpu
from jax.sharding import PartitionSpec as P

NX, NY, NZ = 4, 4, 8
D = 2560
FFB = 192
SFB = 384
TOK = 32
EXPERTS = 64
META = 128
KVW = 1024
KVL = 256
ROW = D + META + KVL
COLS = 512
EPSILON = 1e-05
BF = jnp.bfloat16
F32 = jnp.float32
MESH = pl.DeviceIdType.MESH
COPIES = 128


def mm(a, b):
    return jnp.dot(a, b, preferred_element_type=F32)


def mm_nt(a, b):
    return lax.dot_general(a, b, (((1,), (1,)), ((), ())), preferred_element_type=F32)


def mm_tn(a, b):
    return lax.dot_general(a, b, (((0,), (0,)), ((), ())), preferred_element_type=F32)


def onehot(cond):
    return jnp.where(cond, 1.0, 0.0).astype(BF)


def iota(shape, dim):
    return lax.broadcasted_iota(jnp.int32, shape, dim)


def kernel(
    hidden, gain, router, ids, path, lens, owner, slot, tree,
    eg, eu, ed, sg, su, sd,
    sums, moved,
    zbuf, xsend, ag, outb, rl, rs, sret, ret, ohg, comb, zl, zr,
    shb, outs, rls, rss, hid, hids, kvs, kvr,
    wg0, wu0, wd0, vg0, vu0, vd0, wg1, wu1, wd1, vg1, vu1, vd1,
    send_sem, recv_sem, local_sem,
):
    gx, gy = lax.axis_index("gx"), lax.axis_index("gy")
    y, c = gx // 2, gx % 2
    x, z = gy // NZ, gy % NZ
    zp = (gx, x * NZ + (z + 1) % NZ)
    zm = (gx, x * NZ + (z + NZ - 1) % NZ)
    xp = (gx, (x + 1) % NX * NZ + z)
    xm = (gx, (x + NX - 1) % NX * NZ + z)
    x2 = (gx, (x + 2) % NX * NZ + z)
    yp = ((y + 1) % NY * 2 + c, gy)
    ym = ((y + NY - 1) % NY * 2 + c, gy)
    mate = (y * 2 + 1 - c, gy)

    started = []

    def send(src, dst, device):
        number = len(started)
        copy = pltpu.make_async_remote_copy(
            src_ref=src, dst_ref=dst,
            send_sem=send_sem.at[number], recv_sem=recv_sem.at[number],
            device_id=device, device_id_type=MESH,
        )
        copy.start()
        started.append(copy)
        return copy

    own = []
    for k, (src, dst) in enumerate(
        ((sg, vg0), (su, vu0), (sd, vd0), (eg, wg0), (eu, wu0), (ed, wd0))
    ):
        copy = pltpu.make_async_copy(src, dst, local_sem.at[k])
        copy.start()
        own.append(copy)

    barrier = pltpu.get_barrier_semaphore()
    for device in (zp, zm, xp, xm, x2, yp, ym, mate):
        pl.semaphore_signal(barrier, inc=1, device_id=device, device_id_type=MESH)

    wide = hidden[...].astype(F32)
    scale = lax.rsqrt(jnp.mean(wide * wide, axis=-1, keepdims=True) + EPSILON)
    normed = (wide * scale * gain[...].reshape(1, D)).astype(BF)
    zbuf[0:TOK, 0:D] = normed
    shb[0:TOK, :] = normed
    scores = 1.0 / (1.0 + jnp.exp(-mm_nt(normed, router[...])))
    named = iota((EXPERTS, TOK), 0)
    chosen = named == ids[0:1, :]
    for k in range(1, ids.shape[0]):
        chosen = chosen | (named == ids[k:k + 1, :])
    chosen = onehot(chosen)
    square = iota((EXPERTS, EXPERTS), 0) == iota((EXPERTS, EXPERTS), 1)
    picked = jnp.where(mm_tn(chosen, onehot(square)) > 0.5, scores, 0.0)
    gates = (picked / jnp.sum(picked, axis=-1, keepdims=True)).astype(BF)
    low = iota((EXPERTS, META), 1)
    high = iota((EXPERTS, META), 0)
    meta = mm(gates, onehot(low == high)) + mm_tn(chosen, onehot(low == high + EXPERTS))
    zbuf[0:TOK, D:D + META] = meta.astype(BF)
    row = iota((TOK, 8), 0)
    steps = jnp.sum(
        jnp.where(row // 4 == iota((TOK, 8), 1), path[...].astype(F32), 0.0), axis=1, keepdims=True
    )
    square_row, square_lane = iota((TOK, TOK), 0), iota((TOK, TOK), 1)
    on_path = square_lane.astype(F32) == steps
    rows_kv = jnp.zeros((TOK, KVL), F32)
    for q in range(4):
        rows_kv += mm(onehot(on_path & (square_row % 4 == q)), tree[:, q * KVL:(q + 1) * KVL])
    zbuf[0:TOK, D + META:ROW] = rows_kv.astype(BF)

    pl.semaphore_wait(barrier, 8)

    right, left = {}, {}

    def hop(h):
        for ch in range(2):
            lo = ch * 16
            if h < 4 or ch == 0:
                if h > 1:
                    right[h - 1, ch].wait_recv()
                right[h, ch] = send(
                    zbuf.at[pl.ds((h - 1) * TOK + lo, 16), :], zbuf.at[pl.ds(h * TOK + lo, 16), :], zp
                )
            if h < 4 or ch == 1:
                if h > 1:
                    left[h - 1, ch].wait_recv()
                left[h, ch] = send(
                    zbuf.at[pl.ds((NZ - h + 1) % NZ * TOK + lo, 16), :],
                    zbuf.at[pl.ds((NZ - h) * TOK + lo, 16), :], zm,
                )

    hop(1)
    tokens = zbuf.at[pl.ds(0, TOK), pl.ds(0, D)]
    sh_p = send(tokens, shb.at[pl.ds(TOK, TOK), :], yp)
    sh_m = send(tokens, shb.at[pl.ds(2 * TOK, TOK), :], ym)
    other = [
        send(src, dst, mate)
        for src, dst in ((sg, vg1), (su, vu1), (sd, vd1), (eg, wg1), (eu, wu1), (ed, wd1))
    ]
    hop(2)
    sh_p.wait_recv()
    sh_p2 = send(shb.at[pl.ds(TOK, 16), :], shb.at[pl.ds(3 * TOK, 16), :], yp)
    sh_m.wait_recv()
    sh_m2 = send(shb.at[pl.ds(2 * TOK + 16, 16), :], shb.at[pl.ds(3 * TOK + 16, 16), :], ym)
    hop(3)
    hop(4)
    right[3, 1].wait_recv()
    left[3, 0].wait_recv()
    right[4, 0].wait_recv()
    left[4, 1].wait_recv()

    rows = NZ * TOK
    pair = iota((16, META), 0) % 8
    step = pair // 2
    turn = jnp.where(step == 2, 3, jnp.where(step == 3, 2, step))
    expert = 2 * ((x + turn) % NX * NZ + z) + pair % 2
    meta_lane = iota((16, META), 1)
    all_meta = zbuf[:, D:D + META]
    gate_of = mm_nt(onehot(meta_lane == expert), all_meta)
    mask_of = mm_nt(onehot(meta_lane == expert + EXPERTS), all_meta)
    big_row, big_lane = iota((rows, rows), 0), iota((rows, rows), 1)
    before = onehot((big_row < big_lane) & (big_row // TOK == big_lane // TOK))
    place = mm(mask_of.astype(BF), before)
    key = jnp.where(mask_of > 0.5, place, -1.0)
    slot_row, slot_lane = iota((TOK, rows), 0), iota((TOK, rows), 1)
    block = slot_lane // TOK == slot_row // 4
    seat = (slot_row % 4).astype(F32)

    def slots(i):
        parts = []
        for l in range(2):
            j = 2 * i + l
            here = block & (key[j:j + 1, :] == seat)
            ohg[pl.ds(j * TOK, TOK), :] = jnp.where(here, gate_of[j:j + 1, :], 0.0).astype(BF)
            parts.append(onehot(here))
        return jnp.concatenate(parts, axis=0)

    sent_x = {}
    for i, device in ((3, x2), (1, xp), (2, xm), (0, None)):
        table = slots(i)

        @pl.loop(0, D // COLS)
        def _(n):
            cols = pl.ds(pl.multiple_of(n * COLS, COLS), COLS)
            value = mm(table, zbuf[:, cols]).astype(BF)
            for l in range(2):
                part = value[l * TOK:(l + 1) * TOK, :]
                if i:
                    xsend[i - 1, l, :, cols] = part
                else:
                    ag[l, 0:TOK, cols] = part

        if i:
            for l in range(2):
                sent_x[i, l] = send(xsend.at[i - 1, l], ag.at[l, pl.ds(i * TOK, TOK), :], device)

    direct, relay = {}, {}

    def spread(j):
        for l in range(2):
            here = ag.at[l, pl.ds(j * TOK, TOK), :]
            direct[j, l, 0] = send(here, ag.at[l, pl.ds((NX + j) * TOK, TOK), :], yp)
            direct[j, l, 1] = send(here, ag.at[l, pl.ds((2 * NX + j) * TOK, TOK), :], ym)

    def pass_on(j):
        far = 3 * NX + j
        direct[j, 0, 0].wait_recv()
        relay[j, 0] = send(
            ag.at[0, pl.ds((NX + j) * TOK, TOK), :], ag.at[0, pl.ds(far * TOK, TOK), :], yp
        )
        direct[j, 1, 1].wait_recv()
        relay[j, 1] = send(
            ag.at[1, pl.ds((2 * NX + j) * TOK, TOK), :], ag.at[1, pl.ds(far * TOK, TOK), :], ym
        )

    spread(0)

    kv_row, kv_lane = iota((TOK, rows), 0), iota((TOK, rows), 1)
    spreader = onehot(kv_row == NZ * x + (z + NZ - kv_lane // TOK) % NZ)

    def per_lane(ref):
        return mm(jnp.broadcast_to(ref[...].astype(F32), (16, TOK)).astype(BF), spreader)[0:1, :]

    own_v, slot_v, len_v = per_lane(owner), per_lane(slot), per_lane(lens)
    pick_row, pick_lane = iota((64, rows), 0), iota((64, rows), 1)
    kv_step = pick_row // 16
    kv_turn = jnp.where(kv_step == 2, 3, jnp.where(kv_step == 3, 2, kv_step))
    target = ((x + kv_turn) % NX * NZ + z).astype(F32)
    depth = (pick_lane % TOK // 4).astype(F32)
    wanted = (own_v == target) & (slot_v + depth == (pick_row % 16).astype(F32)) & (depth < len_v)
    for q in range(4):
        value = mm(onehot(wanted & (pick_lane % 4 == q)), zbuf[:, D + META:ROW]).astype(BF)
        for i in range(4):
            kvs[i, :, q * KVL:(q + 1) * KVL] = value[i * 16:(i + 1) * 16, :]
    sent_kv = [
        send(kvs.at[i], kvr.at[i - 1], device) for i, device in ((1, xp), (2, xm), (3, x2))
    ]

    sh_p2.wait_recv()
    sh_m2.wait_recv()
    for k in range(3):
        own[k].wait()
        other[k].wait_recv()

    def silu_mul(g, u):
        return (g / (1.0 + jnp.exp(-g)) * u).astype(BF)

    for h, (vg, vu) in enumerate(((vg0, vu0), (vg1, vu1))):
        hids[h] = silu_mul(mm(shb[...], vg[...]), mm(shb[...], vu[...]))

    @pl.loop(0, D // COLS)
    def _(n):
        cols = pl.ds(pl.multiple_of(n * COLS, COLS), COLS)
        outs[:, cols] = (mm(hids[0], vd0[:, cols]) + mm(hids[1], vd1[:, cols])).astype(BF)

    far_p = send(outs.at[pl.ds(3 * TOK, 16), :], rls.at[0], yp)
    far_m = send(outs.at[pl.ds(3 * TOK + 16, 16), :], rls.at[1], ym)

    for l in range(2):
        sent_x[1, l].wait_recv()
    spread(1)
    pass_on(0)
    for l in range(2):
        sent_x[2, l].wait_recv()
    spread(2)
    pass_on(1)
    for l in range(2):
        sent_x[3, l].wait_recv()
    spread(3)
    far_p.wait_recv()
    outs[2 * TOK:2 * TOK + 16, :] = (
        outs[2 * TOK:2 * TOK + 16, :].astype(F32) + rls[0].astype(F32)
    ).astype(BF)
    far_m.wait_recv()
    outs[TOK + 16:2 * TOK, :] = (
        outs[TOK + 16:2 * TOK, :].astype(F32) + rls[1].astype(F32)
    ).astype(BF)
    back_p = send(outs.at[pl.ds(2 * TOK, TOK), :], rss.at[0], yp)
    back_m = send(outs.at[pl.ds(TOK, TOK), :], rss.at[1], ym)
    pass_on(2)
    pass_on(3)
    for k in range(3, 6):
        own[k].wait()
        other[k].wait_recv()
    for j in range(4):
        direct[j, 1, 0].wait_recv()
        direct[j, 0, 1].wait_recv()

    def routed(first, count):
        @pl.loop(0, 2)
        def _(l):
            for h, (wg, wu) in enumerate(((wg0, wu0), (wg1, wu1))):
                value = ag[l, first:first + count, :]
                hid[h, 0:count, :] = silu_mul(mm_nt(value, wg[l]), mm_nt(value, wu[l]))

            @pl.loop(0, D // COLS)
            def _(n):
                cols = pl.ds(pl.multiple_of(n * COLS, COLS), COLS)
                outb[l, first:first + count, cols] = (
                    mm(hid[0, 0:count, :], wd0[l, :, cols]) + mm(hid[1, 0:count, :], wd1[l, :, cols])
                ).astype(BF)

    span = NX * TOK
    routed(0, 3 * span)
    plain_p = send(outb.at[1, pl.ds(2 * span, span), :], rs.at[0, 1], yp)
    plain_m = send(outb.at[0, pl.ds(span, span), :], rs.at[1, 0], ym)
    for j in range(4):
        relay[j, 0].wait_recv()
        relay[j, 1].wait_recv()
    routed(3 * span, span)

    order = (3, 1, 2, 0)
    far = {}
    for j in order:
        rows_j = pl.ds(3 * span + j * TOK, TOK)
        far[j, 0] = send(outb.at[0, rows_j, :], rl.at[0, pl.ds(j * TOK, TOK), :], yp)
        far[j, 1] = send(outb.at[1, rows_j, :], rl.at[1, pl.ds(j * TOK, TOK), :], ym)
    back = {}
    sent_back = {}

    def add_far(j):
        lo = j * TOK
        for l, base, device in ((0, 2 * span, yp), (1, span, ym)):
            far[j, l].wait_recv()
            outb[l, base + lo:base + lo + TOK, :] = (
                outb[l, base + lo:base + lo + TOK, :].astype(F32) + rl[l, lo:lo + TOK, :].astype(F32)
            ).astype(BF)
            back[j, l] = send(
                outb.at[l, pl.ds(base + lo, TOK), :], rs.at[l, l, pl.ds(lo, TOK), :], device
            )

    def finish(j, device):
        lo = j * TOK
        for l in range(2):
            back[j, l].wait_recv()
        for l in range(2):
            total = (
                outb[l, lo:lo + TOK, :].astype(F32)
                + rs[0, l, lo:lo + TOK, :].astype(F32)
                + rs[1, l, lo:lo + TOK, :].astype(F32)
            ).astype(BF)
            if j:
                sret[l, lo:lo + TOK, :] = total
                sent_back[j, l] = send(
                    sret.at[l, pl.ds(lo, TOK), :], ret.at[pl.ds((2 * j + l) * TOK, TOK), :], device
                )
            else:
                ret[l * TOK:(l + 1) * TOK, :] = total

    goes = {0: None, 1: xm, 2: xp, 3: x2}
    add_far(3)
    plain_p.wait_recv()
    plain_m.wait_recv()
    add_far(1)
    finish(3, goes[3])
    add_far(2)
    finish(1, goes[1])
    add_far(0)
    finish(2, goes[2])
    finish(0, goes[0])
    for copy in sent_back.values():
        copy.wait_recv()

    def combine(k):
        weights = ohg[:, k * TOK:(k + 1) * TOK]

        @pl.loop(0, D // COLS)
        def _(n):
            cols = pl.ds(pl.multiple_of(n * COLS, COLS), COLS)
            comb[k * TOK:(k + 1) * TOK, cols] = mm_tn(weights, ret[:, cols]).astype(BF)

    for k in range(NZ):
        combine(k)
    go_l, go_r = {}, {}
    for h in range(1, 5):
        for ch in range(2):
            lo = ch * 16
            for flow, going, buf, k, device in (
                (0, go_l, zl, 5 - h, zm), (1, go_r, zr, 3 + h, zp)
            ):
                if h == 1 and ch == flow:
                    continue
                at = k * TOK + lo
                if (h - 1, ch) in going:
                    going[h - 1, ch].wait_recv()
                    comb[at:at + 16, :] = (
                        comb[at:at + 16, :].astype(F32) + buf[h - 2, lo:lo + 16, :].astype(F32)
                    ).astype(BF)
                going[h, ch] = send(
                    comb.at[pl.ds(at, 16), :], buf.at[h - 1, pl.ds(lo, 16), :], device
                )

    back_p.wait_recv()
    back_m.wait_recv()
    for copy in sent_kv:
        copy.wait_recv()
    moved[...] = (
        kvs[0].astype(F32) + kvr[0].astype(F32) + kvr[1].astype(F32) + kvr[2].astype(F32)
    ).astype(BF)
    total = outs[0:TOK, :].astype(F32) + rss[0].astype(F32) + rss[1].astype(F32)
    total = total + comb[0:TOK, :].astype(F32)
    for ch in range(2):
        go_l[4, ch].wait_recv()
        go_r[4, ch].wait_recv()
    sums[...] = (total + zl[3].astype(F32) + zr[3].astype(F32)).astype(BF)
    for copy in started:
        copy.wait_send()


def place(sums, moved, out, kept):
    out[...] = sums[...]
    kept[...] = moved[...]


def shards(
    hidden_in, norm_gain, router_weight, expert_ids, expert_gate, expert_up, expert_down,
    shared_gate, shared_up, shared_down, tree_kv, accepted_path, accepted_len, cache_owner, owner_slot,
):
    vmem = pl.BlockSpec(memory_space=pltpu.VMEM)
    hbm = pl.BlockSpec(memory_space=pl.ANY)
    V = pltpu.VMEM
    span = NX * TOK
    scratch = [
        V((NZ * TOK, ROW), BF),
        V((3, 2, TOK, D), BF),
        V((2, NY * span, D), BF),
        V((2, NY * span, D), BF),
        V((2, span, D), BF),
        V((2, 2, span, D), BF),
        V((2, span, D), BF),
        V((2 * span, D), BF),
        V((2 * span, NZ * TOK), BF),
        V((NZ * TOK, D), BF),
        V((4, TOK, D), BF),
        V((4, TOK, D), BF),
        V((NY * TOK, D), BF),
        V((NY * TOK, D), BF),
        V((2, 16, D), BF),
        V((2, TOK, D), BF),
        V((2, 3 * span, FFB), BF),
        V((2, NY * TOK, SFB), BF),
        V((4, 16, KVW), BF),
        V((3, 16, KVW), BF),
    ]
    for _ in range(2):
        scratch += [
            V((2, FFB, D), BF), V((2, FFB, D), BF), V((2, FFB, D), BF),
            V((D, SFB), BF), V((D, SFB), BF), V((SFB, D), BF),
        ]
    scratch += [
        pltpu.SemaphoreType.DMA((COPIES,)),
        pltpu.SemaphoreType.DMA((COPIES,)),
        pltpu.SemaphoreType.DMA((6,)),
    ]
    sums, moved = pl.pallas_call(
        kernel,
        name="verify_ffn",
        out_shape=(
            jax.ShapeDtypeStruct((TOK, D), BF),
            jax.ShapeDtypeStruct((16, KVW), BF),
        ),
        in_specs=[vmem] * 9 + [hbm] * 6,
        out_specs=(vmem, vmem),
        scratch_shapes=scratch,
        compiler_params=pltpu.CompilerParams(
            collective_id=0, has_side_effects=True, vmem_limit_bytes=62 * 1024 * 1024
        ),
    )(
        hidden_in, norm_gain, router_weight.T, expert_ids.T, accepted_path,
        accepted_len.reshape(1, TOK), cache_owner.reshape(1, TOK), owner_slot.reshape(1, TOK), tree_kv,
        expert_gate.swapaxes(1, 2), expert_up.swapaxes(1, 2), expert_down, shared_gate, shared_up, shared_down,
    )
    return pl.pallas_call(
        place,
        name="place",
        out_shape=(
            jax.ShapeDtypeStruct((TOK, D), BF),
            jax.ShapeDtypeStruct((16, KVW), BF),
        ),
        in_specs=[vmem] * 2,
        out_specs=(vmem, vmem),
    )(sums, moved)


def solution(mesh):
    in_specs = (
        P(("gx", "gy"), None),
        P(),
        P(),
        P(("gx", "gy"), None),
        P("gy", None, "gx"),
        P("gy", None, "gx"),
        P("gy", "gx", None),
        P(None, "gx"),
        P(None, "gx"),
        P("gx", None),
        P(("gx", "gy"), None),
        P(("gx", "gy"), None),
        P("gx"),
        P("gx"),
        P("gx"),
    )
    out_specs = (P(("gx", "gy"), None), P(("gx", "gy"), None))
    return jax.shard_map(shards, mesh=mesh, in_specs=in_specs, out_specs=out_specs, check_vma=False)
```

```python
import jax
import jax.numpy as jnp
from jax import lax
from jax.experimental import pallas as pl
from jax.experimental.pallas import tpu as pltpu
from jax.sharding import PartitionSpec as P

NX, NY, NZ = 4, 4, 8
D = 2560
FFB = 192
SFB = 384
TOK = 32
EXPERTS = 64
META = 128
KVW = 1024
KVL = 256
ROW = D + META + KVL
COLS = 512
EPSILON = 1e-05
BF = jnp.bfloat16
F32 = jnp.float32
MESH = pl.DeviceIdType.MESH
COPIES = 128
HALF = 128


def mm(a, b):
    return jnp.dot(a, b, preferred_element_type=F32)


def mm_nt(a, b):
    return lax.dot_general(a, b, (((1,), (1,)), ((), ())), preferred_element_type=F32)


def mm_tn(a, b):
    return lax.dot_general(a, b, (((0,), (0,)), ((), ())), preferred_element_type=F32)


def home(k):
    return (k + 1) % NZ * TOK


def onehot(cond):
    return jnp.where(cond, 1.0, 0.0).astype(BF)


def iota(shape, dim):
    return lax.broadcasted_iota(jnp.int32, shape, dim)


def kernel(
    hidden, gain, router, ids, path, lens, owner, slot, tree,
    eg, eu, ed, sg, su, sd,
    sums, moved,
    zbuf, xsend, ag, outb, rl, rs, sret, ret, ohg, comb, zl, zr,
    shb, outs, rls, rss, hid, hids, kvs, kvr,
    wg0, wu0, wd0, vg0, vu0, vd0, wg1, wu1, wd1, vg1, vu1, vd1,
    send_sem, recv_sem, local_sem,
):
    gx, gy = lax.axis_index("gx"), lax.axis_index("gy")
    y, c = gx // 2, gx % 2
    x, z = gy // NZ, gy % NZ
    zp = (gx, x * NZ + (z + 1) % NZ)
    zm = (gx, x * NZ + (z + NZ - 1) % NZ)
    xp = (gx, (x + 1) % NX * NZ + z)
    xm = (gx, (x + NX - 1) % NX * NZ + z)
    x2 = (gx, (x + 2) % NX * NZ + z)
    yp = ((y + 1) % NY * 2 + c, gy)
    ym = ((y + NY - 1) % NY * 2 + c, gy)
    mate = (y * 2 + 1 - c, gy)

    started = []

    def send(src, dst, device):
        number = len(started)
        copy = pltpu.make_async_remote_copy(
            src_ref=src, dst_ref=dst,
            send_sem=send_sem.at[number], recv_sem=recv_sem.at[number],
            device_id=device, device_id_type=MESH,
        )
        copy.start()
        started.append(copy)
        return copy

    own = []
    for k, (src, dst) in enumerate(
        ((sg, vg0), (su, vu0), (sd, vd0), (eg, wg0), (eu, wu0), (ed, wd0))
    ):
        copy = pltpu.make_async_copy(src, dst, local_sem.at[k])
        copy.start()
        own.append(copy)

    barrier = pltpu.get_barrier_semaphore()
    for device in (zp, zm, xp, xm, x2, yp, ym, mate):
        pl.semaphore_signal(barrier, inc=1, device_id=device, device_id_type=MESH)

    wide = hidden[...].astype(F32)
    scale = lax.rsqrt(jnp.mean(wide * wide, axis=-1, keepdims=True) + EPSILON)
    normed = (wide * scale * gain[...].reshape(1, D)).astype(BF)
    zbuf[TOK:2 * TOK, 0:D] = normed
    shb[0:TOK, :] = normed
    scores = 1.0 / (1.0 + jnp.exp(-mm_nt(normed, router[...])))
    named = iota((EXPERTS, TOK), 0)
    chosen = named == ids[0:1, :]
    for k in range(1, ids.shape[0]):
        chosen = chosen | (named == ids[k:k + 1, :])
    chosen = onehot(chosen)
    square = iota((EXPERTS, EXPERTS), 0) == iota((EXPERTS, EXPERTS), 1)
    picked = jnp.where(mm_tn(chosen, onehot(square)) > 0.5, scores, 0.0)
    gates = (picked / jnp.sum(picked, axis=-1, keepdims=True)).astype(BF)
    low = iota((EXPERTS, META), 1)
    high = iota((EXPERTS, META), 0)
    meta = mm(gates, onehot(low == high)) + mm_tn(chosen, onehot(low == high + EXPERTS))
    zbuf[TOK:2 * TOK, D:D + META] = meta.astype(BF)
    row = iota((TOK, 8), 0)
    steps = jnp.sum(
        jnp.where(row // 4 == iota((TOK, 8), 1), path[...].astype(F32), 0.0), axis=1, keepdims=True
    )
    square_row, square_lane = iota((TOK, TOK), 0), iota((TOK, TOK), 1)
    on_path = square_lane.astype(F32) == steps
    rows_kv = jnp.zeros((TOK, KVL), F32)
    for q in range(4):
        rows_kv += mm(onehot(on_path & (square_row % 4 == q)), tree[:, q * KVL:(q + 1) * KVL])
    zbuf[TOK:2 * TOK, D + META:ROW] = rows_kv.astype(BF)

    pl.semaphore_wait(barrier, 8)

    right, left = {}, {}

    def hop(h):
        for ch in range(2):
            lo = ch * 16
            if h < 4 or ch == 0:
                if h > 1:
                    right[h - 1, ch].wait_recv()
                right[h, ch] = send(
                    zbuf.at[pl.ds(home(h - 1) + lo, 16), :], zbuf.at[pl.ds(home(h) + lo, 16), :], zp
                )
            if h < 4 or ch == 1:
                if h > 1:
                    left[h - 1, ch].wait_recv()
                left[h, ch] = send(
                    zbuf.at[pl.ds(home(1 - h) + lo, 16), :], zbuf.at[pl.ds(home(-h) + lo, 16), :], zm
                )

    hop(1)
    tokens = shb.at[pl.ds(0, TOK), :]
    sh_p = send(tokens, shb.at[pl.ds(TOK, TOK), :], yp)
    sh_m = send(tokens, shb.at[pl.ds(2 * TOK, TOK), :], ym)
    other = [
        send(src, dst, mate)
        for src, dst in ((sg, vg1), (su, vu1), (sd, vd1), (eg, wg1), (eu, wu1), (ed, wd1))
    ]
    hop(2)
    sh_p.wait_recv()
    sh_p2 = send(shb.at[pl.ds(TOK, 16), :], shb.at[pl.ds(3 * TOK, 16), :], yp)
    sh_m.wait_recv()
    sh_m2 = send(shb.at[pl.ds(2 * TOK + 16, 16), :], shb.at[pl.ds(3 * TOK + 16, 16), :], ym)
    hop(3)

    pair = iota((16, META), 0) % 8
    step = pair // 2
    turn = jnp.where(step == 2, 3, jnp.where(step == 3, 2, step))
    expert = 2 * ((x + turn) % NX * NZ + z) + pair % 2
    meta_lane = iota((16, META), 1)
    gate_pick = onehot(meta_lane == expert)
    mask_pick = onehot(meta_lane == expert + EXPERTS)
    sq_row, sq_lane = iota((HALF, HALF), 0), iota((HALF, HALF), 1)
    before = onehot((sq_row < sq_lane) & (sq_row // TOK == sq_lane // TOK))
    widen = onehot(iota((HALF, 16), 0) // 16 == iota((HALF, 16), 1))
    block = sq_lane // TOK == sq_row % 16 // 4
    seat = (sq_row % 4).astype(F32)
    sent_x = {}

    def slots(g):
        base = g * HALF
        all_meta = zbuf[base:base + HALF, D:D + META]
        gate_of = mm_nt(gate_pick, all_meta).astype(BF)
        mask_of = mm_nt(mask_pick, all_meta)
        order = mm(mask_of.astype(BF), before)
        key = mm(widen, jnp.where(mask_of > 0.5, order, -1.0).astype(BF))
        here = block & (key == seat)
        ohg[g] = jnp.where(here, mm(widen, gate_of), 0.0).T.astype(BF)
        table = onehot(here)

        @pl.loop(0, D // COLS)
        def _(n):
            cols = pl.ds(pl.multiple_of(n * COLS, COLS), COLS)
            value = mm(table, zbuf[base:base + HALF, cols]).astype(BF)
            for l in range(2):
                ag[l, g * 256:g * 256 + 16, cols] = value[l * 16:(l + 1) * 16, :]
            for j in range(2, 8):
                xsend[g, j - 2, :, cols] = value[j * 16:(j + 1) * 16, :]

        for i, device in ((3, x2), (1, xp), (2, xm)):
            sent_x[g, i] = send(
                xsend.at[g, pl.ds(2 * i - 2, 2)], ag.at[:, pl.ds(g * 256 + i * 16, 16), :], device
            )

    direct, relay = {}, {}

    def spread(g, j):
        if j:
            sent_x[g, j].wait_recv()
        at = g * 256 + j * 16
        here = ag.at[:, pl.ds(at, 16), :]
        direct[g, j, 0] = send(here, ag.at[:, pl.ds(at + 64, 16), :], yp)
        direct[g, j, 1] = send(here, ag.at[:, pl.ds(at + 128, 16), :], ym)

    def pass_on(g, j):
        at = g * 256 + j * 16
        for l, device in ((0, yp), (1, ym)):
            direct[g, j, l].wait_recv()
            relay[g, j, l] = send(
                ag.at[l, pl.ds(at + 64 * (l + 1), 16), :], ag.at[l, pl.ds(at + 192, 16), :], device
            )

    slots(0)
    spread(0, 0)
    hop(4)
    spread(0, 1)
    spread(0, 2)
    pass_on(0, 0)
    right[3, 1].wait_recv()
    left[3, 0].wait_recv()
    right[4, 0].wait_recv()
    left[4, 1].wait_recv()
    slots(1)
    spread(0, 3)
    spread(1, 0)
    pass_on(0, 1)
    pass_on(0, 2)

    rows = NZ * TOK
    kv_row, kv_lane = iota((TOK, rows), 0), iota((TOK, rows), 1)
    spreader = onehot(kv_row == NZ * x + (z + NZ + 1 - kv_lane // TOK) % NZ)

    def per_lane(ref):
        return mm(jnp.broadcast_to(ref[...].astype(F32), (16, TOK)).astype(BF), spreader)[0:1, :]

    own_v, slot_v, len_v = per_lane(owner), per_lane(slot), per_lane(lens)
    pick_row, pick_lane = iota((64, rows), 0), iota((64, rows), 1)
    kv_step = pick_row // 16
    kv_turn = jnp.where(kv_step == 2, 3, jnp.where(kv_step == 3, 2, kv_step))
    target = ((x + kv_turn) % NX * NZ + z).astype(F32)
    depth = (pick_lane % TOK // 4).astype(F32)
    wanted = (own_v == target) & (slot_v + depth == (pick_row % 16).astype(F32)) & (depth < len_v)
    for q in range(4):
        value = mm(onehot(wanted & (pick_lane % 4 == q)), zbuf[:, D + META:ROW]).astype(BF)
        for i in range(4):
            kvs[i, :, q * KVL:(q + 1) * KVL] = value[i * 16:(i + 1) * 16, :]
    sent_kv = [
        send(kvs.at[i], kvr.at[i - 1], device) for i, device in ((1, xp), (2, xm), (3, x2))
    ]

    sh_p2.wait_recv()
    sh_m2.wait_recv()
    for k in range(3):
        own[k].wait()
        other[k].wait_recv()

    def silu_mul(g, u):
        return (g / (1.0 + jnp.exp(-g)) * u).astype(BF)

    for h, (vg, vu) in enumerate(((vg0, vu0), (vg1, vu1))):
        hids[h] = silu_mul(mm(shb[...], vg[...]), mm(shb[...], vu[...]))

    @pl.loop(0, D // COLS)
    def _(n):
        cols = pl.ds(pl.multiple_of(n * COLS, COLS), COLS)
        outs[:, cols] = (mm(hids[0], vd0[:, cols]) + mm(hids[1], vd1[:, cols])).astype(BF)

    far_p = send(outs.at[pl.ds(3 * TOK, 16), :], rls.at[0], yp)
    far_m = send(outs.at[pl.ds(3 * TOK + 16, 16), :], rls.at[1], ym)

    spread(1, 1)
    spread(1, 2)
    pass_on(0, 3)
    spread(1, 3)
    far_p.wait_recv()
    outs[2 * TOK:2 * TOK + 16, :] = (
        outs[2 * TOK:2 * TOK + 16, :].astype(F32) + rls[0].astype(F32)
    ).astype(BF)
    far_m.wait_recv()
    outs[TOK + 16:2 * TOK, :] = (
        outs[TOK + 16:2 * TOK, :].astype(F32) + rls[1].astype(F32)
    ).astype(BF)
    back_p = send(outs.at[pl.ds(2 * TOK, TOK), :], rss.at[0], yp)
    back_m = send(outs.at[pl.ds(TOK, TOK), :], rss.at[1], ym)
    for k in range(3, 6):
        own[k].wait()
        other[k].wait_recv()

    def routed(g):
        for j in range(4):
            for l in range(2):
                relay[g, j, l].wait_recv()

        @pl.loop(0, 2)
        def _(l):
            for h, (wg, wu) in enumerate(((wg0, wu0), (wg1, wu1))):
                value = ag[l, g * 256:(g + 1) * 256, :]
                hid[h] = silu_mul(mm_nt(value, wg[l]), mm_nt(value, wu[l]))

            @pl.loop(0, D // COLS)
            def _(n):
                cols = pl.ds(pl.multiple_of(n * COLS, COLS), COLS)
                outb[l, g * 256:(g + 1) * 256, cols] = (
                    mm(hid[0], wd0[l, :, cols]) + mm(hid[1], wd1[l, :, cols])
                ).astype(BF)

    far, plain, back, sent_back = {}, {}, {}, {}
    order = (3, 1, 2, 0)

    def send_far(g):
        for j in order:
            at = pl.ds(g * 256 + 192 + j * 16, 16)
            to = pl.ds(g * 64 + j * 16, 16)
            far[g, j, 0] = send(outb.at[0, at, :], rl.at[0, to, :], yp)
            far[g, j, 1] = send(outb.at[1, at, :], rl.at[1, to, :], ym)

    def send_plain(g):
        to = pl.ds(g * 64, 64)
        plain[g, 0] = send(outb.at[1, pl.ds(g * 256 + 128, 64), :], rs.at[0, 1, to, :], yp)
        plain[g, 1] = send(outb.at[0, pl.ds(g * 256 + 64, 64), :], rs.at[1, 0, to, :], ym)

    def add_far(g, j):
        lo = g * 64 + j * 16
        for l, base, device in ((0, 128, yp), (1, 64, ym)):
            far[g, j, l].wait_recv()
            at = g * 256 + base + j * 16
            outb[l, at:at + 16, :] = (
                outb[l, at:at + 16, :].astype(F32) + rl[l, lo:lo + 16, :].astype(F32)
            ).astype(BF)
            back[g, j, l] = send(outb.at[l, pl.ds(at, 16), :], rs.at[l, l, pl.ds(lo, 16), :], device)

    goes = {1: xm, 2: xp, 3: x2}

    def finish(g, j):
        lo, at = g * 64 + j * 16, g * 256 + j * 16
        for l in range(2):
            back[g, j, l].wait_recv()
        for l in range(2):
            total = (
                outb[l, at:at + 16, :].astype(F32)
                + rs[0, l, lo:lo + 16, :].astype(F32)
                + rs[1, l, lo:lo + 16, :].astype(F32)
            ).astype(BF)
            if j:
                sret[g, 2 * j - 2 + l] = total
            else:
                ret[g, l] = total
        if j:
            sent_back[g, j] = send(
                sret.at[g, pl.ds(2 * j - 2, 2)], ret.at[g, pl.ds(2 * j, 2)], goes[j]
            )

    def combine(g):
        for j in (3, 1, 2):
            sent_back[g, j].wait_recv()
        weights = ohg[g]

        @pl.loop(0, D // COLS)
        def _(n):
            cols = pl.ds(pl.multiple_of(n * COLS, COLS), COLS)
            value = ret[g, :, :, cols].reshape(HALF, COLS)
            comb[g * HALF:(g + 1) * HALF, cols] = mm(weights, value).astype(BF)

    go_l, go_r = {}, {}

    def fold(flow, h):
        going, buf, k, device = (
            (go_r, zr, 3 + h, zp) if flow else (go_l, zl, 5 - h, zm)
        )
        for ch in range(2):
            if h == 1 and ch == flow:
                continue
            lo = ch * 16
            at = home(k) + lo
            if (h - 1, ch) in going:
                going[h - 1, ch].wait_recv()
                comb[at:at + 16, :] = (
                    comb[at:at + 16, :].astype(F32) + buf[h - 2, lo:lo + 16, :].astype(F32)
                ).astype(BF)
            going[h, ch] = send(
                comb.at[pl.ds(at, 16), :], buf.at[h - 1, pl.ds(lo, 16), :], device
            )

    routed(0)
    send_far(0)
    for j in range(4):
        pass_on(1, j)
    send_plain(0)
    routed(1)
    send_far(1)
    send_plain(1)
    for j in order:
        add_far(1, j)
    plain[0, 0].wait_recv()
    plain[0, 1].wait_recv()
    plain[1, 0].wait_recv()
    plain[1, 1].wait_recv()
    for j in order:
        add_far(0, j)
        finish(1, j)
    combine(1)
    fold(0, 1)
    fold(1, 1)
    finish(0, 3)
    fold(0, 2)
    fold(1, 2)
    finish(0, 1)
    finish(0, 2)
    fold(1, 3)
    finish(0, 0)
    combine(0)
    fold(0, 3)
    fold(1, 4)
    fold(0, 4)

    back_p.wait_recv()
    back_m.wait_recv()
    for copy in sent_kv:
        copy.wait_recv()
    moved[...] = (
        kvs[0].astype(F32) + kvr[0].astype(F32) + kvr[1].astype(F32) + kvr[2].astype(F32)
    ).astype(BF)
    total = outs[0:TOK, :].astype(F32) + rss[0].astype(F32) + rss[1].astype(F32)
    total = total + comb[home(0):home(0) + TOK, :].astype(F32)
    for ch in range(2):
        go_l[4, ch].wait_recv()
        go_r[4, ch].wait_recv()
    sums[...] = (total + zl[3].astype(F32) + zr[3].astype(F32)).astype(BF)
    for copy in started:
        copy.wait_send()


def place(sums, moved, out, kept):
    out[...] = sums[...]
    kept[...] = moved[...]


def shards(
    hidden_in, norm_gain, router_weight, expert_ids, expert_gate, expert_up, expert_down,
    shared_gate, shared_up, shared_down, tree_kv, accepted_path, accepted_len, cache_owner, owner_slot,
):
    vmem = pl.BlockSpec(memory_space=pltpu.VMEM)
    hbm = pl.BlockSpec(memory_space=pl.ANY)
    V = pltpu.VMEM
    span = NX * TOK
    scratch = [
        V((NZ * TOK, ROW), BF),
        V((2, 6, 16, D), BF),
        V((2, NY * span, D), BF),
        V((2, NY * span, D), BF),
        V((2, span, D), BF),
        V((2, 2, span, D), BF),
        V((2, 6, 16, D), BF),
        V((2, 8, 16, D), BF),
        V((2, HALF, HALF), BF),
        V((NZ * TOK, D), BF),
        V((4, TOK, D), BF),
        V((4, TOK, D), BF),
        V((NY * TOK, D), BF),
        V((NY * TOK, D), BF),
        V((2, 16, D), BF),
        V((2, TOK, D), BF),
        V((2, 2 * span, FFB), BF),
        V((2, NY * TOK, SFB), BF),
        V((4, 16, KVW), BF),
        V((3, 16, KVW), BF),
    ]
    for _ in range(2):
        scratch += [
            V((2, FFB, D), BF), V((2, FFB, D), BF), V((2, FFB, D), BF),
            V((D, SFB), BF), V((D, SFB), BF), V((SFB, D), BF),
        ]
    scratch += [
        pltpu.SemaphoreType.DMA((COPIES,)),
        pltpu.SemaphoreType.DMA((COPIES,)),
        pltpu.SemaphoreType.DMA((6,)),
    ]
    sums, moved = pl.pallas_call(
        kernel,
        name="verify_ffn",
        out_shape=(
            jax.ShapeDtypeStruct((TOK, D), BF),
            jax.ShapeDtypeStruct((16, KVW), BF),
        ),
        in_specs=[vmem] * 9 + [hbm] * 6,
        out_specs=(vmem, vmem),
        scratch_shapes=scratch,
        compiler_params=pltpu.CompilerParams(
            collective_id=0, has_side_effects=True, vmem_limit_bytes=62 * 1024 * 1024
        ),
    )(
        hidden_in, norm_gain, router_weight.T, expert_ids.T, accepted_path,
        accepted_len.reshape(1, TOK), cache_owner.reshape(1, TOK), owner_slot.reshape(1, TOK), tree_kv,
        expert_gate.swapaxes(1, 2), expert_up.swapaxes(1, 2), expert_down, shared_gate, shared_up, shared_down,
    )
    return pl.pallas_call(
        place,
        name="place",
        out_shape=(
            jax.ShapeDtypeStruct((TOK, D), BF),
            jax.ShapeDtypeStruct((16, KVW), BF),
        ),
        in_specs=[vmem] * 2,
        out_specs=(vmem, vmem),
    )(sums, moved)


def solution(mesh):
    in_specs = (
        P(("gx", "gy"), None),
        P(),
        P(),
        P(("gx", "gy"), None),
        P("gy", None, "gx"),
        P("gy", None, "gx"),
        P("gy", "gx", None),
        P(None, "gx"),
        P(None, "gx"),
        P("gx", None),
        P(("gx", "gy"), None),
        P(("gx", "gy"), None),
        P("gx"),
        P("gx"),
        P("gx"),
    )
    out_specs = (P(("gx", "gy"), None), P(("gx", "gy"), None))
    return jax.shard_map(shards, mesh=mesh, in_specs=in_specs, out_specs=out_specs, check_vma=False)
```

```python
import jax
import jax.numpy as jnp
from jax import lax
from jax.experimental import pallas as pl
from jax.experimental.pallas import tpu as pltpu
from jax.sharding import PartitionSpec as P

NX, NY, NZ = 4, 4, 8
D = 2560
FFB = 192
SFB = 384
TOK = 32
EXPERTS = 64
META = 128
KVW = 1024
KVL = 256
KB = 768
KA = D - KB
ROW = KA + META + KVL
COLS = 512
PART = 256
EPSILON = 1e-05
BF = jnp.bfloat16
F32 = jnp.float32
MESH = pl.DeviceIdType.MESH
COPIES = 192
HALF = 128


def mm(a, b):
    return jnp.dot(a, b, preferred_element_type=F32)


def mm_nt(a, b):
    return lax.dot_general(a, b, (((1,), (1,)), ((), ())), preferred_element_type=F32)


def mm_tn(a, b):
    return lax.dot_general(a, b, (((0,), (0,)), ((), ())), preferred_element_type=F32)


def place_of(k):
    return (k + 1) % NZ


def home(k):
    return (k + 1) % NZ * TOK


def onehot(cond):
    return jnp.where(cond, 1.0, 0.0).astype(BF)


def iota(shape, dim):
    return lax.broadcasted_iota(jnp.int32, shape, dim)


def kernel(
    hidden, gain, router, ids, path, lens, owner, slot, tree,
    eg, eu, ed, sg, su, sd,
    sums, moved,
    zbuf, xsend, ag, outb, rl, rs, sret, ret, ohg, comb, zl, zr,
    shb, outs, rls, rss, hid, hids, kvs, kvr,
    zb, xsend_b, ret_b, comb_b, zl_b, zr_b, ohg_b,
    wg0, wu0, wd0, vg0, vu0, vd0, wg1, wu1, wd1, vg1, vu1, vd1,
    send_sem, recv_sem, local_sem,
):
    gx, gy = lax.axis_index("gx"), lax.axis_index("gy")
    y, c = gx // 2, gx % 2
    x, z = gy // NZ, gy % NZ
    zp = (gx, x * NZ + (z + 1) % NZ)
    zm = (gx, x * NZ + (z + NZ - 1) % NZ)
    xp = (gx, (x + 1) % NX * NZ + z)
    xm = (gx, (x + NX - 1) % NX * NZ + z)
    x2 = (gx, (x + 2) % NX * NZ + z)
    yp = ((y + 1) % NY * 2 + c, gy)
    ym = ((y + NY - 1) % NY * 2 + c, gy)
    mate = (y * 2 + 1 - c, gy)

    started = []

    def send(src, dst, device):
        number = len(started)
        copy = pltpu.make_async_remote_copy(
            src_ref=src, dst_ref=dst,
            send_sem=send_sem.at[number], recv_sem=recv_sem.at[number],
            device_id=device, device_id_type=MESH,
        )
        copy.start()
        started.append(copy)
        return copy

    own = []
    for k, (src, dst) in enumerate(
        ((sg, vg0), (su, vu0), (sd, vd0), (eg, wg0), (eu, wu0), (ed, wd0))
    ):
        copy = pltpu.make_async_copy(src, dst, local_sem.at[k])
        copy.start()
        own.append(copy)

    barrier = pltpu.get_barrier_semaphore()
    for device in (zp, zm, xp, xm, x2, yp, ym, mate):
        pl.semaphore_signal(barrier, inc=1, device_id=device, device_id_type=MESH)

    wide = hidden[...].astype(F32)
    scale = lax.rsqrt(jnp.mean(wide * wide, axis=-1, keepdims=True) + EPSILON)
    normed = (wide * scale * gain[...].reshape(1, D)).astype(BF)
    zbuf[TOK:2 * TOK, 0:KA] = normed[:, 0:KA]
    shb[0:TOK, 0:D] = normed
    scores = 1.0 / (1.0 + jnp.exp(-mm_nt(normed, router[...])))
    named = iota((EXPERTS, TOK), 0)
    chosen = named == ids[0:1, :]
    for k in range(1, ids.shape[0]):
        chosen = chosen | (named == ids[k:k + 1, :])
    chosen = onehot(chosen)
    square = iota((EXPERTS, EXPERTS), 0) == iota((EXPERTS, EXPERTS), 1)
    picked = jnp.where(mm_tn(chosen, onehot(square)) > 0.5, scores, 0.0)
    gates = (picked / jnp.sum(picked, axis=-1, keepdims=True)).astype(BF)
    low = iota((EXPERTS, META), 1)
    high = iota((EXPERTS, META), 0)
    meta = mm(gates, onehot(low == high)) + mm_tn(chosen, onehot(low == high + EXPERTS))
    meta = meta.astype(BF)
    zbuf[TOK:2 * TOK, KA:KA + META] = meta
    shb[0:TOK, D:D + META] = meta
    row = iota((TOK, 8), 0)
    steps = jnp.sum(
        jnp.where(row // 4 == iota((TOK, 8), 1), path[...].astype(F32), 0.0), axis=1, keepdims=True
    )
    square_row, square_lane = iota((TOK, TOK), 0), iota((TOK, TOK), 1)
    on_path = square_lane.astype(F32) == steps
    rows_kv = jnp.zeros((TOK, KVL), F32)
    for q in range(4):
        rows_kv += mm(onehot(on_path & (square_row % 4 == q)), tree[:, q * KVL:(q + 1) * KVL])
    zbuf[TOK:2 * TOK, KA + META:ROW] = rows_kv.astype(BF)

    pl.semaphore_wait(barrier, 8)

    right, left = {}, {}

    def hop(h):
        for ch in range(2):
            lo = ch * 16
            if h < 4 or ch == 0:
                if h > 1:
                    right[h - 1, ch].wait_recv()
                right[h, ch] = send(
                    zbuf.at[pl.ds(home(h - 1) + lo, 16), :], zbuf.at[pl.ds(home(h) + lo, 16), :], zp
                )
            if h < 4 or ch == 1:
                if h > 1:
                    left[h - 1, ch].wait_recv()
                left[h, ch] = send(
                    zbuf.at[pl.ds(home(1 - h) + lo, 16), :], zbuf.at[pl.ds(home(-h) + lo, 16), :], zm
                )

    right_b, left_b = {}, {}

    def hop_b(h):
        for ch in range(2):
            part = pl.ds(2 * ch, 2)
            if h < 4 or ch == 0:
                if h > 1:
                    right_b[h - 1, ch].wait_recv()
                right_b[h, ch] = send(zb.at[place_of(h - 1), part], zb.at[place_of(h), part], zp)
            if h < 4 or ch == 1:
                if h > 1:
                    left_b[h - 1, ch].wait_recv()
                left_b[h, ch] = send(zb.at[place_of(1 - h), part], zb.at[place_of(-h), part], zm)

    hop(1)
    sh_p = send(shb.at[pl.ds(0, TOK), :], shb.at[pl.ds(TOK, TOK), :], yp)
    sh_m = send(shb.at[pl.ds(0, TOK), :], shb.at[pl.ds(2 * TOK, TOK), :], ym)
    other = [
        send(src, dst, mate)
        for src, dst in ((sg, vg1), (su, vu1), (sd, vd1), (eg, wg1), (eu, wu1), (ed, wd1))
    ]
    hop(2)
    sh_p.wait_recv()
    sh_p2 = send(shb.at[pl.ds(TOK, 16), :], shb.at[pl.ds(3 * TOK, 16), :], yp)
    sh_m.wait_recv()
    sh_m2 = send(shb.at[pl.ds(2 * TOK + 16, 16), :], shb.at[pl.ds(3 * TOK + 16, 16), :], ym)
    hop(3)

    pair = iota((16, META), 0) % 8
    step = pair // 2
    turn = jnp.where(step == 2, 3, jnp.where(step == 3, 2, step))
    expert = 2 * ((x + turn) % NX * NZ + z) + pair % 2
    meta_lane = iota((16, META), 1)
    gate_pick = onehot(meta_lane == expert)
    mask_pick = onehot(meta_lane == expert + EXPERTS)
    sq_row, sq_lane = iota((HALF, HALF), 0), iota((HALF, HALF), 1)
    before = onehot((sq_row < sq_lane) & (sq_row // TOK == sq_lane // TOK))
    widen = onehot(iota((HALF, 16), 0) // 16 == iota((HALF, 16), 1))
    block = sq_lane // TOK == sq_row % 16 // 4
    seat = (sq_row % 4).astype(F32)
    sent_x = {}

    def tables(all_meta):
        gate_of = mm_nt(gate_pick, all_meta).astype(BF)
        mask_of = mm_nt(mask_pick, all_meta)
        order = mm(mask_of.astype(BF), before)
        key = mm(widen, jnp.where(mask_of > 0.5, order, -1.0).astype(BF))
        here = block & (key == seat)
        return onehot(here), jnp.where(here, mm(widen, gate_of), 0.0).T.astype(BF)

    def slots(g):
        base = g * HALF
        table, ohg[g] = tables(zbuf[base:base + HALF, KA:KA + META])

        @pl.loop(0, KA // PART)
        def _(n):
            cols = pl.ds(pl.multiple_of(n * PART, PART), PART)
            value = mm(table, zbuf[base:base + HALF, cols]).astype(BF)
            for l in range(2):
                ag[l, 4 * g, 0:16, cols] = value[l * 16:(l + 1) * 16, :]
            for j in range(2, 8):
                xsend[g, j - 2, :, cols] = value[j * 16:(j + 1) * 16, :]

        for i, device in ((3, x2), (1, xp), (2, xm)):
            sent_x[g, i] = send(
                xsend.at[g, pl.ds(2 * i - 2, 2)],
                ag.at[:, 4 * g, pl.ds(i * 16, 16), pl.ds(0, KA)], device,
            )

    sent_xb = {}

    def slots_b(g):
        homes = slice(4 * g, 4 * g + 4)

        @pl.loop(0, NY)
        def _(r):
            table, ohg_b[g, r] = tables(zb[homes, r, :, KB:KB + META].reshape(HALF, META))

            @pl.loop(0, KB // PART)
            def _(n):
                at = pl.multiple_of(n * PART, PART)
                cols = pl.ds(at, PART)
                value = mm(table, zb[homes, r, :, cols].reshape(HALF, PART)).astype(BF)
                for l in range(2):
                    ag[l, 4 * g + r, 0:16, pl.ds(KA + at, PART)] = value[l * 16:(l + 1) * 16, :]
                for j in range(2, 8):
                    xsend_b[g, j - 2, r, :, cols] = value[j * 16:(j + 1) * 16, :]

        for i, device in ((3, x2), (1, xp), (2, xm)):
            sent_xb[g, i] = send(
                xsend_b.at[g, pl.ds(2 * i - 2, 2)],
                ag.at[:, pl.ds(4 * g, 4), pl.ds(i * 16, 16), pl.ds(KA, KB)], device,
            )

    direct, relay = {}, {}

    def spread(g, j):
        if j:
            sent_x[g, j].wait_recv()
        at, cols = pl.ds(j * 16, 16), pl.ds(0, KA)
        here = ag.at[:, 4 * g, at, cols]
        direct[g, j, 0] = send(here, ag.at[:, 4 * g + 1, at, cols], yp)
        direct[g, j, 1] = send(here, ag.at[:, 4 * g + 2, at, cols], ym)

    def pass_on(g, j):
        at, cols = pl.ds(j * 16, 16), pl.ds(0, KA)
        for l, device in ((0, yp), (1, ym)):
            direct[g, j, l].wait_recv()
            relay[g, j, l] = send(
                ag.at[l, 4 * g + l + 1, at, cols], ag.at[l, 4 * g + 3, at, cols], device
            )

    slots(0)
    spread(0, 0)
    hop(4)
    sh_p2.wait_recv()
    sh_m2.wait_recv()
    for r in range(NY):
        zb[place_of(0), r] = shb[r * TOK:(r + 1) * TOK, KA:D + META]
    hop_b(1)
    spread(0, 1)
    spread(0, 2)
    pass_on(0, 0)
    right[3, 1].wait_recv()
    left[3, 0].wait_recv()
    right[4, 0].wait_recv()
    left[4, 1].wait_recv()
    slots(1)
    spread(0, 3)
    spread(1, 0)
    hop_b(2)
    pass_on(0, 1)
    pass_on(0, 2)
    hop_b(3)
    slots_b(0)
    spread(1, 1)
    spread(1, 2)
    pass_on(0, 3)
    spread(1, 3)
    hop_b(4)

    rows = NZ * TOK
    kv_row, kv_lane = iota((TOK, rows), 0), iota((TOK, rows), 1)
    spreader = onehot(kv_row == NZ * x + (z + NZ + 1 - kv_lane // TOK) % NZ)

    def per_lane(ref):
        return mm(jnp.broadcast_to(ref[...].astype(F32), (16, TOK)).astype(BF), spreader)[0:1, :]

    own_v, slot_v, len_v = per_lane(owner), per_lane(slot), per_lane(lens)
    pick_row, pick_lane = iota((64, rows), 0), iota((64, rows), 1)
    kv_step = pick_row // 16
    kv_turn = jnp.where(kv_step == 2, 3, jnp.where(kv_step == 3, 2, kv_step))
    target = ((x + kv_turn) % NX * NZ + z).astype(F32)
    depth = (pick_lane % TOK // 4).astype(F32)
    wanted = (own_v == target) & (slot_v + depth == (pick_row % 16).astype(F32)) & (depth < len_v)
    for q in range(4):
        value = mm(onehot(wanted & (pick_lane % 4 == q)), zbuf[:, KA + META:ROW]).astype(BF)
        for i in range(4):
            kvs[i, :, q * KVL:(q + 1) * KVL] = value[i * 16:(i + 1) * 16, :]
    sent_kv = [
        send(kvs.at[i], kvr.at[i - 1], device) for i, device in ((1, xp), (2, xm), (3, x2))
    ]

    for k in range(3):
        own[k].wait()
        other[k].wait_recv()

    def silu_mul(g, u):
        return (g / (1.0 + jnp.exp(-g)) * u).astype(BF)

    for h, (vg, vu) in enumerate(((vg0, vu0), (vg1, vu1))):
        hids[h] = silu_mul(mm(shb[:, 0:D], vg[...]), mm(shb[:, 0:D], vu[...]))

    @pl.loop(0, D // COLS)
    def _(n):
        cols = pl.ds(pl.multiple_of(n * COLS, COLS), COLS)
        outs[:, cols] = (mm(hids[0], vd0[:, cols]) + mm(hids[1], vd1[:, cols])).astype(BF)

    def shared_far(cols):
        return (
            send(outs.at[pl.ds(3 * TOK, 16), cols], rls.at[0, :, cols], yp),
            send(outs.at[pl.ds(3 * TOK + 16, 16), cols], rls.at[1, :, cols], ym),
        )

    def shared_back(parts, cols):
        parts[0].wait_recv()
        outs[2 * TOK:2 * TOK + 16, cols] = (
            outs[2 * TOK:2 * TOK + 16, cols].astype(F32) + rls[0, :, cols].astype(F32)
        ).astype(BF)
        parts[1].wait_recv()
        outs[TOK + 16:2 * TOK, cols] = (
            outs[TOK + 16:2 * TOK, cols].astype(F32) + rls[1, :, cols].astype(F32)
        ).astype(BF)
        return (
            send(outs.at[pl.ds(2 * TOK, TOK), cols], rss.at[0, :, cols], yp),
            send(outs.at[pl.ds(TOK, TOK), cols], rss.at[1, :, cols], ym),
        )

    cols_a, cols_b = pl.ds(0, KA), pl.ds(KA, KB)
    shared_a = shared_far(cols_a)
    pass_on(1, 0)
    pass_on(1, 1)
    right_b[3, 1].wait_recv()
    left_b[3, 0].wait_recv()
    right_b[4, 0].wait_recv()
    left_b[4, 1].wait_recv()
    slots_b(1)
    shared_a = shared_back(shared_a, cols_a)
    pass_on(1, 2)
    pass_on(1, 3)
    for k in range(3, 6):
        own[k].wait()
        other[k].wait_recv()

    def routed(g):
        for j in range(4):
            for l in range(2):
                relay[g, j, l].wait_recv()
        for i in (3, 1, 2):
            sent_xb[g, i].wait_recv()

        @pl.loop(0, 2)
        def _(l):
            for h, (wg, wu) in enumerate(((wg0, wu0), (wg1, wu1))):
                value = ag[l, 4 * g:4 * g + 4].reshape(256, D)
                hid[h] = silu_mul(mm_nt(value, wg[l]), mm_nt(value, wu[l]))

            @pl.loop(0, D // COLS)
            def _(n):
                cols = pl.ds(pl.multiple_of(n * COLS, COLS), COLS)
                outb[l, 4 * g:4 * g + 4, :, cols] = (
                    mm(hid[0], wd0[l, :, cols]) + mm(hid[1], wd1[l, :, cols])
                ).astype(BF).reshape(4, 64, COLS)

    far, plain, back, sent_back = {}, {}, {}, {}
    order = (3, 1, 2, 0)

    def send_far(g):
        for j in order:
            at = pl.ds(j * 16, 16)
            to = pl.ds(g * 64 + j * 16, 16)
            far[g, j, 0] = send(outb.at[0, 4 * g + 3, at, cols_a], rl.at[0, to, :], yp)
            far[g, j, 1] = send(outb.at[1, 4 * g + 3, at, cols_a], rl.at[1, to, :], ym)

    def send_plain(g):
        to = pl.ds(g * 64, 64)
        plain[g, 0] = send(outb.at[1, 4 * g + 2, :, cols_a], rs.at[0, 1, to, :], yp)
        plain[g, 1] = send(outb.at[0, 4 * g + 1, :, cols_a], rs.at[1, 0, to, :], ym)

    def add_far(g, j):
        lo, at = g * 64 + j * 16, j * 16
        for l, r, device in ((0, 2, yp), (1, 1, ym)):
            far[g, j, l].wait_recv()
            outb[l, 4 * g + r, at:at + 16, 0:KA] = (
                outb[l, 4 * g + r, at:at + 16, 0:KA].astype(F32) + rl[l, lo:lo + 16, :].astype(F32)
            ).astype(BF)
            back[g, j, l] = send(
                outb.at[l, 4 * g + r, pl.ds(at, 16), cols_a], rs.at[l, l, pl.ds(lo, 16), :], device
            )

    goes = {1: xm, 2: xp, 3: x2}

    def finish(g, j):
        lo, at = g * 64 + j * 16, j * 16
        for l in range(2):
            back[g, j, l].wait_recv()
        for l in range(2):
            total = (
                outb[l, 4 * g, at:at + 16, 0:KA].astype(F32)
                + rs[0, l, lo:lo + 16, :].astype(F32)
                + rs[1, l, lo:lo + 16, :].astype(F32)
            ).astype(BF)
            if j:
                sret[g, 2 * j - 2 + l] = total
            else:
                ret[g, l] = total
        if j:
            sent_back[g, j] = send(
                sret.at[g, pl.ds(2 * j - 2, 2)], ret.at[g, pl.ds(2 * j, 2)], goes[j]
            )

    back_b = {}

    def return_b(g):
        for j in order[:3]:
            back_b[g, j] = send(
                outb.at[:, pl.ds(4 * g, 4), pl.ds(j * 16, 16), cols_b], ret_b.at[g, pl.ds(2 * j, 2)], goes[j]
            )
        ret_b[g, 0:2] = outb[:, 4 * g:4 * g + 4, 0:16, KA:D]

    def combine(g):
        for j in (3, 1, 2):
            sent_back[g, j].wait_recv()
        weights = ohg[g]

        @pl.loop(0, KA // PART)
        def _(n):
            cols = pl.ds(pl.multiple_of(n * PART, PART), PART)
            value = ret[g, :, :, cols].reshape(HALF, PART)
            comb[g * HALF:(g + 1) * HALF, cols] = mm(weights, value).astype(BF)

    def combine_b(g):
        for j in (3, 1, 2):
            back_b[g, j].wait_recv()

        @pl.loop(0, NY)
        def _(r):
            weights = ohg_b[g, r]

            @pl.loop(0, KB // PART)
            def _(n):
                cols = pl.ds(pl.multiple_of(n * PART, PART), PART)
                value = ret_b[g, :, r, :, cols].reshape(HALF, PART)
                comb_b[4 * g:4 * g + 4, r, :, cols] = (
                    mm(weights, value).astype(BF).reshape(4, TOK, PART)
                )

    go_lb, go_rb = {}, {}

    def fold_b(flow, h):
        going, buf, k, device = (
            (go_rb, zr_b, 3 + h, zp) if flow else (go_lb, zl_b, 5 - h, zm)
        )
        m = place_of(k)
        for ch in range(2):
            if h == 1 and ch == flow:
                continue
            part = pl.ds(2 * ch, 2)
            if (h - 1, ch) in going:
                going[h - 1, ch].wait_recv()
                comb_b[m, part] = (
                    comb_b[m, part].astype(F32) + buf[h - 2, part].astype(F32)
                ).astype(BF)
            going[h, ch] = send(comb_b.at[m, part], buf.at[h - 1, part], device)

    go_l, go_r = {}, {}

    def fold(flow, h):
        going, buf, k, device = (
            (go_r, zr, 3 + h, zp) if flow else (go_l, zl, 5 - h, zm)
        )
        for ch in range(2):
            if h == 1 and ch == flow:
                continue
            lo = ch * 16
            at = home(k) + lo
            if (h - 1, ch) in going:
                going[h - 1, ch].wait_recv()
                comb[at:at + 16, :] = (
                    comb[at:at + 16, :].astype(F32) + buf[h - 2, lo:lo + 16, :].astype(F32)
                ).astype(BF)
            going[h, ch] = send(
                comb.at[pl.ds(at, 16), :], buf.at[h - 1, pl.ds(lo, 16), :], device
            )

    routed(0)
    return_b(0)
    send_far(0)
    send_plain(0)
    routed(1)
    return_b(1)
    send_far(1)
    send_plain(1)
    combine_b(0)
    for j in order:
        add_far(1, j)
    for j in order:
        add_far(0, j)
    combine_b(1)
    fold_b(0, 1)
    fold_b(1, 1)
    for g in range(2):
        for k in range(2):
            plain[g, k].wait_recv()
    finish(1, 3)
    finish(1, 1)
    fold_b(0, 2)
    fold_b(1, 2)
    finish(1, 2)
    finish(1, 0)
    combine(1)
    fold(0, 1)
    fold(1, 1)
    fold_b(0, 3)
    fold_b(1, 3)
    finish(0, 3)
    finish(0, 1)
    fold(0, 2)
    fold(1, 2)
    finish(0, 2)
    finish(0, 0)
    fold_b(0, 4)
    fold_b(1, 4)
    fold(1, 3)
    combine(0)
    fold(0, 3)
    fold(1, 4)
    for ch in range(2):
        go_lb[4, ch].wait_recv()
        go_rb[4, ch].wait_recv()
    outs[:, KA:D] = (
        outs[:, KA:D].astype(F32)
        + (
            comb_b[place_of(0)].astype(F32) + zl_b[3].astype(F32) + zr_b[3].astype(F32)
        ).reshape(NY * TOK, KB)
    ).astype(BF)
    shared_b = shared_far(cols_b)
    fold(0, 4)
    for copy in sent_kv:
        copy.wait_recv()
    moved[...] = (
        kvs[0].astype(F32) + kvr[0].astype(F32) + kvr[1].astype(F32) + kvr[2].astype(F32)
    ).astype(BF)
    shared_b = shared_back(shared_b, cols_b)
    for copy in shared_a:
        copy.wait_recv()
    for ch in range(2):
        go_l[4, ch].wait_recv()
        go_r[4, ch].wait_recv()
    total = outs[0:TOK, 0:KA].astype(F32) + rss[0, :, 0:KA].astype(F32) + rss[1, :, 0:KA].astype(F32)
    total = total + comb[home(0):home(0) + TOK, :].astype(F32)
    sums[:, 0:KA] = (total + zl[3].astype(F32) + zr[3].astype(F32)).astype(BF)
    for copy in shared_b:
        copy.wait_recv()
    sums[:, KA:D] = (
        outs[0:TOK, KA:D].astype(F32) + rss[0, :, KA:D].astype(F32) + rss[1, :, KA:D].astype(F32)
    ).astype(BF)
    for copy in started:
        copy.wait_send()


def place(sums, moved, out, kept):
    out[...] = sums[...]
    kept[...] = moved[...]


def shards(
    hidden_in, norm_gain, router_weight, expert_ids, expert_gate, expert_up, expert_down,
    shared_gate, shared_up, shared_down, tree_kv, accepted_path, accepted_len, cache_owner, owner_slot,
):
    vmem = pl.BlockSpec(memory_space=pltpu.VMEM)
    hbm = pl.BlockSpec(memory_space=pl.ANY)
    V = pltpu.VMEM
    span = NX * TOK
    scratch = [
        V((NZ * TOK, ROW), BF),
        V((2, 6, 16, KA), BF),
        V((2, 2 * NY, 64, D), BF),
        V((2, 2 * NY, 64, D), BF),
        V((2, span, KA), BF),
        V((2, 2, span, KA), BF),
        V((2, 6, 16, KA), BF),
        V((2, 8, 16, KA), BF),
        V((2, HALF, HALF), BF),
        V((NZ * TOK, KA), BF),
        V((4, TOK, KA), BF),
        V((4, TOK, KA), BF),
        V((NY * TOK, D + META), BF),
        V((NY * TOK, D), BF),
        V((2, 16, D), BF),
        V((2, TOK, D), BF),
        V((2, 2 * span, FFB), BF),
        V((2, NY * TOK, SFB), BF),
        V((4, 16, KVW), BF),
        V((3, 16, KVW), BF),
        V((NZ, NY, TOK, KB + META), BF),
        V((2, 6, NY, 16, KB), BF),
        V((2, 8, NY, 16, KB), BF),
        V((NZ, NY, TOK, KB), BF),
        V((4, NY, TOK, KB), BF),
        V((4, NY, TOK, KB), BF),
        V((2, NY, HALF, HALF), BF),
    ]
    for _ in range(2):
        scratch += [
            V((2, FFB, D), BF), V((2, FFB, D), BF), V((2, FFB, D), BF),
            V((D, SFB), BF), V((D, SFB), BF), V((SFB, D), BF),
        ]
    scratch += [
        pltpu.SemaphoreType.DMA((COPIES,)),
        pltpu.SemaphoreType.DMA((COPIES,)),
        pltpu.SemaphoreType.DMA((6,)),
    ]
    sums, moved = pl.pallas_call(
        kernel,
        name="verify_ffn",
        out_shape=(
            jax.ShapeDtypeStruct((TOK, D), BF),
            jax.ShapeDtypeStruct((16, KVW), BF),
        ),
        in_specs=[vmem] * 9 + [hbm] * 6,
        out_specs=(vmem, vmem),
        scratch_shapes=scratch,
        compiler_params=pltpu.CompilerParams(
            collective_id=0, has_side_effects=True, vmem_limit_bytes=62 * 1024 * 1024
        ),
    )(
        hidden_in, norm_gain, router_weight.T, expert_ids.T, accepted_path,
        accepted_len.reshape(1, TOK), cache_owner.reshape(1, TOK), owner_slot.reshape(1, TOK), tree_kv,
        expert_gate.swapaxes(1, 2), expert_up.swapaxes(1, 2), expert_down, shared_gate, shared_up, shared_down,
    )
    return pl.pallas_call(
        place,
        name="place",
        out_shape=(
            jax.ShapeDtypeStruct((TOK, D), BF),
            jax.ShapeDtypeStruct((16, KVW), BF),
        ),
        in_specs=[vmem] * 2,
        out_specs=(vmem, vmem),
    )(sums, moved)


def solution(mesh):
    in_specs = (
        P(("gx", "gy"), None),
        P(),
        P(),
        P(("gx", "gy"), None),
        P("gy", None, "gx"),
        P("gy", None, "gx"),
        P("gy", "gx", None),
        P(None, "gx"),
        P(None, "gx"),
        P("gx", None),
        P(("gx", "gy"), None),
        P(("gx", "gy"), None),
        P("gx"),
        P("gx"),
        P("gx"),
    )
    out_specs = (P(("gx", "gy"), None), P(("gx", "gy"), None))
    return jax.shard_map(shards, mesh=mesh, in_specs=in_specs, out_specs=out_specs, check_vma=False)
```
